32 devices in a mesh: gx: 4 (over x, core), gy: 8 (over z, y).
Axes of the slice: x: 2, y: 2, z: 4, core: 2. Of those that a mesh axis runs over, the one named last changes fastest.
Arguments:
- rock_rhs: float32 [128, 128, 128], P('gx', 'gy'), may hold values from -6 to 6
- frac_rhs: float32 [1024, 4096], P(('gx', 'gy')), may hold values from -6 to 6
- perm: float32 [128, 128, 128], P('gx', 'gy'), may hold values from 0.1 to 10
- storage: float32 [128, 128, 128], P('gx', 'gy'), may hold values from 0.002 to 0.05
- pressure: float32 [128, 128, 128], P('gx', 'gy'), may hold values from -4 to 4
- frac_perm: float32 [1024, 4096], P(('gx', 'gy')), may hold values from 0.5 to 20
- frac_storage: float32 [1024, 4096], P(('gx', 'gy')), may hold values from 0.002 to 0.05
- frac_pressure: float32 [1024, 4096], P(('gx', 'gy')), may hold values from -4 to 4
- couple_geom: float32 [1024, 128], P(('gx', 'gy')), may hold values from 0.1 to 2
- couple_count: int32 [1024], P(('gx', 'gy')), may hold values from 1 to 128, as said below
- couple_frac_cell: int32 [1024, 128], P(('gx', 'gy')), may hold values from 0 to 4095
- couple_rock_cell: int32 [1024, 128], P(('gx', 'gy')), may hold values from 0 to 65535
- host_offset: int32 [1024], P(('gx', 'gy')), may hold values from -1 to 1, as said below
- cross_pairs: int32 [2, 8192], P(None, ('gx', 'gy')), may hold values from 0 to 131071, as said below
- cross_geom: float32 [8192], P(('gx', 'gy')), may hold values from 0.1 to 2
- aggregates: int32 [128, 128, 128], P('gx', 'gy'), may hold values from 0 to 63, as said below
Outputs:
- rock_update: float32 [128, 128, 128], P('gx', 'gy')
- frac_update: float32 [1024, 4096], P(('gx', 'gy'))
- residual_norm: float32 [], replicated
The draws below stay inside these ranges and needn't reach their ends.
Inputs may be any that keep to these rules, and one draw needn't show every extreme that they name: `couple_count`: every fracture has at least one live slot, and in every draw some fracture fills all 128. `host_offset`: the host block always exists: owners at the first gy index never have -1, owners at the last never +1. `cross_pairs`: cells are numbered within the owner device's 32 fractures, 4096 each; the two ends of a pair lie in different fractures. `aggregates`: each aggregate is a face-connected set of cells inside one device's block; every one of the 64 numbers is used in every block, with counts that differ from block to block.
All inputs are finite; a program needn't handle non-finite values.
Results may differ from the reference program's by a relative error of at most 0.0003.
Values sent between devices are 32-bit elements; how exact they have to be, the bound alone decides.
No kernel may reach another device: no remote copies, remote signals or barrier semaphores. Data moves between devices by JAX's collectives and lax.ppermute only.
A program may use at most 128 MiB of HBM per device.

```python
import math
import jax
import jax.numpy as jnp
from jax import lax

CX = 32
CY = 16
NZ = 128
FR_DEV = 32
IX_DEV = 256
FSIDE = 64
KC = 128
NAGG = 64
ITERS = 2
NX = 128
NY = 128
FRACS = 1024
IXS = 8192
N_GX = 4
N_GY = 8


def draw_couple_count(key, part):
    counts = jax.random.randint(jax.random.fold_in(key, 11), (FRACS,), 1, KC + 1)
    full_at = jax.random.randint(jax.random.fold_in(key, 12), (), 0, FRACS)
    hop_at = jax.random.randint(jax.random.fold_in(key, 13), (), 1, FRACS)
    counts = counts.at[full_at].set(KC)
    counts = counts.at[(full_at + hop_at) % FRACS].set(1)
    return counts.astype(jnp.int32)


def draw_host_offset(key, part):
    offsets = jax.random.randint(jax.random.fold_in(key, 21), (FRACS,), -1, 2)
    lanes = NY // CY
    owner_y = jnp.arange(FRACS, dtype=jnp.int32) // FR_DEV % lanes
    offsets = jnp.where(owner_y == 0, jnp.maximum(offsets, 0), offsets)
    offsets = jnp.where(owner_y == lanes - 1, jnp.minimum(offsets, 0), offsets)
    return offsets.astype(jnp.int32)


def draw_cross_pairs(key, part):
    span = FR_DEV * FSIDE * FSIDE
    former = jax.random.randint(jax.random.fold_in(key, 31), (IXS,), 0, span)
    jumps = jax.random.randint(jax.random.fold_in(key, 32), (IXS,), 1, FR_DEV)
    latter = (former + jumps * FSIDE * FSIDE) % span
    return jnp.stack([former, latter]).astype(jnp.int32)


def draw_aggregates(key, part):
    blocks_x = NX // CX
    blocks_y = NY // CY
    total = CX * CY * NZ
    stride = total // NAGG
    jitter = stride // 4
    cell_x = lax.broadcasted_iota(jnp.int32, (CX, CY, NZ), 0)
    cell_y = lax.broadcasted_iota(jnp.int32, (CX, CY, NZ), 1)
    cell_z = lax.broadcasted_iota(jnp.int32, (CX, CY, NZ), 2)
    turned_y = jnp.where(cell_x % 2 == 0, cell_y, CY - 1 - cell_y)
    lane = cell_x * CY + turned_y
    turned_z = jnp.where(lane % 2 == 0, cell_z, NZ - 1 - cell_z)
    position = (lane * NZ + turned_z).reshape(-1)
    shifts = jax.random.randint(jax.random.fold_in(key, 41), (blocks_x * blocks_y, NAGG - 1), -jitter, jitter + 1)
    cuts = (jnp.arange(1, NAGG, dtype=jnp.int32) * stride)[None, :] + shifts
    labels = jax.vmap(lambda row: jnp.searchsorted(row, position, side='right'))(cuts)
    labels = labels.reshape(blocks_x, blocks_y, CX, CY, NZ).transpose(0, 2, 1, 3, 4)
    return labels.reshape(NX, NY, NZ).astype(jnp.int32)


def place_ends(values, own_key, least, top_value):
    longest = values.shape.index(max(values.shape))
    spots = []
    for shift in (0, 1):
        where = [jax.random.randint(jax.random.fold_in(own_key, axis), (), 0, length) for axis, length in enumerate(values.shape)]
        where[longest] = (where[longest] + shift) % values.shape[longest]
        spots.append(tuple(where))
    return values.at[spots[0]].set(least).at[spots[1]].set(top_value)


def level_of(stream_key, dims, split, smallest, largest):
    def one(dim, shards_of):
        draws = jax.random.uniform(jax.random.fold_in(jax.random.fold_in(stream_key, 6), dim), (shards_of,), jnp.float32, smallest / len(split), largest / len(split))
        return jnp.repeat(jnp.exp(draws), dims[dim] // shards_of).reshape((-1,) + (1,) * (len(dims) - dim - 1))

    level = one(*split[0])
    for cut in split[1:]:
        level = level * one(*cut)
    return level


def scatter_about(rng, extent, deviation, limit, shards=(), kind=jnp.bfloat16):
    drawn = deviation * jax.random.normal(rng, extent, jnp.float32)
    if shards:
        drawn = drawn * level_of(rng, extent, shards, -0.22, 0.18)
    return jnp.clip(drawn, -limit, limit).astype(kind)


def setup_inputs(seed: int = 0) -> dict:
    streams_of = jax.random.split(jax.random.key(seed), 17)
    rock_rhs = scatter_about(streams_of[0], (NX, NY, NZ), 1.0, 6.0, ((0, 4), (1, 8)), jnp.float32)
    frac_rhs = scatter_about(streams_of[1], (FRACS, FSIDE * FSIDE), 1.0, 6.0, ((0, 32),), jnp.float32)
    perm = jnp.clip(jnp.exp(math.log(10.0) - 4.6051702 * jax.random.uniform(streams_of[2], (NX, NY, NZ), jnp.float32) ** level_of(streams_of[2], (NX, NY, NZ), ((0, 4), (1, 8)), -0.2, 0.2)), 0.1, 10.0)
    storage = jnp.clip(jnp.exp(math.log(0.05) - 3.218876 * jax.random.uniform(streams_of[3], (NX, NY, NZ), jnp.float32) ** level_of(streams_of[3], (NX, NY, NZ), ((0, 4), (1, 8)), -0.2, 0.2)), 0.002, 0.05)
    pressure = scatter_about(streams_of[4], (NX, NY, NZ), 1.0, 4.0, ((0, 4), (1, 8)), jnp.float32)
    frac_perm = jnp.clip(jnp.exp(math.log(20.0) - 3.6888795 * jax.random.uniform(streams_of[5], (FRACS, FSIDE * FSIDE), jnp.float32) ** level_of(streams_of[5], (FRACS, FSIDE * FSIDE), ((0, 32),), -0.2, 0.2)), 0.5, 20.0)
    frac_storage = jnp.clip(jnp.exp(math.log(0.05) - 3.218876 * jax.random.uniform(streams_of[6], (FRACS, FSIDE * FSIDE), jnp.float32) ** level_of(streams_of[6], (FRACS, FSIDE * FSIDE), ((0, 32),), -0.2, 0.2)), 0.002, 0.05)
    frac_pressure = scatter_about(streams_of[7], (FRACS, FSIDE * FSIDE), 1.0, 4.0, ((0, 32),), jnp.float32)
    couple_geom = jnp.clip(jnp.exp(math.log(2.0) - 2.9957323 * jax.random.uniform(streams_of[8], (FRACS, KC), jnp.float32) ** level_of(streams_of[8], (FRACS, KC), ((0, 32),), -0.2, 0.2)), 0.1, 2.0)
    couple_count = draw_couple_count(jax.random.fold_in(streams_of[16], 71), 0)
    couple_frac_cell = place_ends(jax.random.randint(streams_of[10], (FRACS, KC), 0, FSIDE * FSIDE), jax.random.fold_in(streams_of[10], 1), 0, (FSIDE * FSIDE) - 1).astype(jnp.int32)
    couple_rock_cell = place_ends(jax.random.randint(streams_of[11], (FRACS, KC), 0, CX * CY * NZ), jax.random.fold_in(streams_of[11], 1), 0, (CX * CY * NZ) - 1).astype(jnp.int32)
    host_offset = draw_host_offset(jax.random.fold_in(streams_of[16], 71), 0)
    cross_pairs = draw_cross_pairs(jax.random.fold_in(streams_of[16], 71), 0)
    cross_geom = jnp.clip(jnp.exp(math.log(2.0) - 2.9957323 * jax.random.uniform(streams_of[14], (IXS,), jnp.float32) ** level_of(streams_of[14], (IXS,), ((0, 32),), -0.2, 0.2)), 0.1, 2.0)
    aggregates = draw_aggregates(jax.random.fold_in(streams_of[16], 71), 0)
    return dict(rock_rhs=rock_rhs, frac_rhs=frac_rhs, perm=perm, storage=storage, pressure=pressure, frac_perm=frac_perm, frac_storage=frac_storage, frac_pressure=frac_pressure, couple_geom=couple_geom, couple_count=couple_count, couple_frac_cell=couple_frac_cell, couple_rock_cell=couple_rock_cell, host_offset=host_offset, cross_pairs=cross_pairs, cross_geom=cross_geom, aggregates=aggregates)


mobility_rate = 0.5
relaxation = 0.8
epsilon = 1e-06

def harmonic(former, latter):
    return 2.0 * former * latter / (former + latter)

def mobility(former, latter):
    return jnp.exp(-mobility_rate * 0.5 * (former + latter))

def neighbours(padded):
    return [padded[2:, 1:-1, 1:-1], padded[:-2, 1:-1, 1:-1], padded[1:-1, 2:, 1:-1], padded[1:-1, :-2, 1:-1], padded[1:-1, 1:-1, 2:], padded[1:-1, 1:-1, :-2]]

def fracture_faces(conduct, frac_press):
    column = lax.broadcasted_iota(jnp.int32, conduct.shape, 1)
    along = column % FSIDE
    across = column // FSIDE
    t_along = jnp.where(along < FSIDE - 1, harmonic(conduct, jnp.roll(conduct, -1, 1)) * mobility(frac_press, jnp.roll(frac_press, -1, 1)), 0.0)
    t_across = jnp.where(across < FSIDE - 1, harmonic(conduct, jnp.roll(conduct, -FSIDE, 1)) * mobility(frac_press, jnp.roll(frac_press, -FSIDE, 1)), 0.0)
    return [t_along, jnp.roll(t_along, 1, 1), t_across, jnp.roll(t_across, FSIDE, 1)]

def fracture_stencil(face_list, frac_diag, vector):
    result = frac_diag * vector
    for weight, stride in zip(face_list, (-1, 1, -FSIDE, FSIDE)):
        result = result - weight * jnp.roll(vector, stride, 1)
    return result

def givens_solve(columns, start_norm):
    small_rhs = [start_norm] + [jnp.zeros((), jnp.float32) for column in range(len(columns))]
    rotations = []
    upper = []
    for column, entries in enumerate(columns):
        entries = list(entries)
        for earlier, (cosine, sine) in enumerate(rotations):
            former, latter = (entries[earlier], entries[earlier + 1])
            entries[earlier] = cosine * former + sine * latter
            entries[earlier + 1] = -sine * former + cosine * latter
        radius = jnp.sqrt(entries[column] * entries[column] + entries[column + 1] * entries[column + 1])
        cosine = entries[column] / radius
        sine = entries[column + 1] / radius
        entries[column] = radius
        rotations.append((cosine, sine))
        small_rhs[column + 1] = -sine * small_rhs[column]
        small_rhs[column] = cosine * small_rhs[column]
        upper.append(entries[:column + 1])
    count = len(columns)
    coeffs = [None] * count
    for column in range(count - 1, -1, -1):
        total = small_rhs[column]
        for later in range(column + 1, count):
            total = total - upper[later][column] * coeffs[later]
        coeffs[column] = total / upper[column][column]
    return (coeffs, jnp.abs(small_rhs[count]))

def reference(rock_rhs, frac_rhs, perm, storage, pressure, frac_perm, frac_storage, frac_pressure, couple_geom, couple_count, couple_frac_cell, couple_rock_cell, host_offset, cross_pairs, cross_geom, aggregates):
    fcells = FSIDE * FSIDE
    cell_count = NX * NY * NZ
    devices = N_GX * N_GY
    weights = [harmonic(perm, near_perm) * mobility(pressure, near_press) for near_perm, near_press in zip(neighbours(jnp.pad(perm, 1)), neighbours(jnp.pad(pressure, 1)))]
    face_list = fracture_faces(frac_perm, frac_pressure)
    slot_ids = lax.broadcasted_iota(jnp.int32, (FRACS, KC), 1)
    row_ids = lax.broadcasted_iota(jnp.int32, (FRACS, KC), 0)
    live_mask = slot_ids < couple_count[:, None]
    frac_value = jnp.take_along_axis(frac_pressure, couple_frac_cell, axis=1)
    coupling = jnp.where(live_mask, couple_geom * jnp.exp(-mobility_rate * frac_value), 0.0)
    owner = jnp.arange(FRACS, dtype=jnp.int32) // FR_DEV
    owner_x = owner // N_GY
    host_y = owner % N_GY + host_offset
    local_x = couple_rock_cell // (CY * NZ)
    local_y = couple_rock_cell // NZ % CY
    local_z = couple_rock_cell % NZ
    global_cell = ((owner_x[:, None] * CX + local_x) * NY + host_y[:, None] * CY + local_y) * NZ + local_z
    base = jnp.arange(IXS, dtype=jnp.int32) // IX_DEV * (FR_DEV * fcells)
    former_cell = cross_pairs[0] + base
    latter_cell = cross_pairs[1] + base
    press_flat = frac_pressure.reshape(-1)
    cross_coef = cross_geom * mobility(press_flat[former_cell], press_flat[latter_cell])
    cross_sum = jnp.zeros((FRACS * fcells,), jnp.float32).at[former_cell].add(cross_coef).at[latter_cell].add(cross_coef)
    couple_frac_sum = jnp.zeros((FRACS, fcells), jnp.float32).at[row_ids, couple_frac_cell].add(coupling)
    frac_diag = frac_storage + sum(face_list) + couple_frac_sum + cross_sum.reshape(FRACS, fcells)
    couple_rock_sum = jnp.zeros((cell_count,), jnp.float32).at[global_cell].add(coupling).reshape(NX, NY, NZ)
    rock_diag = storage + sum(weights) + couple_rock_sum

    def rock_part(rock_vec, frac_vec):
        result = rock_diag * rock_vec
        for weight, near in zip(weights, neighbours(jnp.pad(rock_vec, 1))):
            result = result - weight * near
        flux = coupling * jnp.take_along_axis(frac_vec, couple_frac_cell, axis=1)
        return result - jnp.zeros((cell_count,), jnp.float32).at[global_cell].add(flux).reshape(NX, NY, NZ)

    def frac_part(rock_vec, frac_vec):
        result = fracture_stencil(face_list, frac_diag, frac_vec)
        host_value = rock_vec.reshape(-1)[global_cell]
        result = result - jnp.zeros((FRACS, fcells), jnp.float32).at[row_ids, couple_frac_cell].add(coupling * host_value)
        flat = frac_vec.reshape(-1)
        crossing = jnp.zeros((FRACS * fcells,), jnp.float32).at[former_cell].add(cross_coef * flat[latter_cell]).at[latter_cell].add(cross_coef * flat[former_cell])
        return result - crossing.reshape(FRACS, fcells)
    grid_x = lax.broadcasted_iota(jnp.int32, (NX, NY, NZ), 0)
    grid_y = lax.broadcasted_iota(jnp.int32, (NX, NY, NZ), 1)
    global_agg = (grid_x // CX * N_GY + grid_y // CY) * NAGG + aggregates
    coarse_cell = rock_diag
    for weight, near in zip(weights, neighbours(jnp.pad(global_agg, 1, constant_values=-1))):
        coarse_cell = coarse_cell - jnp.where(near == global_agg, weight, 0.0)
    segments = NAGG * devices
    agg_flat = global_agg.reshape(-1)
    coarse_diag = jax.ops.segment_sum(coarse_cell.reshape(-1), agg_flat, num_segments=segments)

    def precond(rock_vec, frac_vec):
        smooth_rock = relaxation * rock_vec / rock_diag
        smooth_frac = relaxation * frac_vec / frac_diag
        leftover = rock_vec - rock_part(smooth_rock, smooth_frac)
        coarse_rhs = jax.ops.segment_sum(leftover.reshape(-1), agg_flat, num_segments=segments)
        coarse_sol = coarse_rhs / coarse_diag
        return (smooth_rock + coarse_sol[global_agg], smooth_frac)

    def inner(former, latter):
        return jnp.sum(former[0] * latter[0]) + jnp.sum(former[1] * latter[1])
    rhs_pair = (rock_rhs, frac_rhs)
    start_norm = jnp.sqrt(inner(rhs_pair, rhs_pair) + epsilon)
    krylov = [(rock_rhs / start_norm, frac_rhs / start_norm)]
    directions = []
    columns = []
    for column in range(ITERS):
        direction = precond(*krylov[-1])
        directions.append(direction)
        image = (rock_part(*direction), frac_part(*direction))
        projections = [inner(image, vector) for vector in krylov]
        for coeff, vector in zip(projections, krylov):
            image = (image[0] - coeff * vector[0], image[1] - coeff * vector[1])
        next_norm = jnp.sqrt(inner(image, image) + epsilon)
        krylov.append((image[0] / next_norm, image[1] / next_norm))
        columns.append(projections + [next_norm])
    coeffs, residual_norm = givens_solve(columns, start_norm)
    rock_update = sum((coeff * direction[0] for coeff, direction in zip(coeffs, directions)))
    frac_update = sum((coeff * direction[1] for coeff, direction in zip(coeffs, directions)))
    return (rock_update, frac_update, residual_norm)
```

```python
import functools

import jax
import jax.numpy as jnp
from jax import lax
from jax.experimental import pallas as pl
from jax.experimental.pallas import tpu as pltpu
from jax.sharding import PartitionSpec as P

FSIDE = 64
NAGG = 64
LANES = 128
GROUP = 4

mobility_rate = 0.5
relaxation = 0.8
epsilon = 1e-06
F32 = jnp.float32
BF16 = jnp.bfloat16
NT = (((1,), (1,)), ((), ()))
TN = (((0,), (0,)), ((), ()))
VM = pl.BlockSpec(memory_space=pltpu.VMEM)
SM = pl.BlockSpec(memory_space=pltpu.SMEM)


def call(kernel, outs, ins, scratch=(), flops=1 << 24, smem_in=(), smem_out=()):
    nbytes = sum(a.size * a.dtype.itemsize for a in list(ins) + list(outs))
    return pl.pallas_call(
        kernel,
        out_shape=tuple(outs),
        in_specs=[SM if i in smem_in else VM for i in range(len(ins))],
        out_specs=tuple(SM if i in smem_out else VM for i in range(len(outs))),
        scratch_shapes=list(scratch),
        cost_estimate=pl.CostEstimate(flops=flops, bytes_accessed=nbytes, transcendentals=0),
    )(*ins)


def shaped(*dims, dtype=F32):
    return jax.ShapeDtypeStruct(dims, dtype)


def swap_pairs(n):
    even = [(i, i ^ 1) for i in range(n) if i ^ 1 < n]
    odd = [(i, ((i - 1) ^ 1) + 1) for i in range(1, n) if ((i - 1) ^ 1) + 1 < n]
    return even, odd


def exchange(even_msg, odd_msg, axis):
    even, odd = swap_pairs(lax.axis_size(axis))
    return lax.ppermute(even_msg, axis, even), lax.ppermute(odd_msg, axis, odd)


def halves(value):
    high = value.astype(BF16)
    return high, (value - high.astype(F32)).astype(BF16)


def thirds(value):
    high = value.astype(BF16)
    rest = value - high.astype(F32)
    mid = rest.astype(BF16)
    return high, mid, (rest - mid.astype(F32)).astype(BF16)


def mm(lhs, rhs, dims):
    return lax.dot_general(lhs, rhs, dims, preferred_element_type=F32)


def iota(shape, dim):
    return lax.broadcasted_iota(jnp.int32, shape, dim)


def lane_pick(table, index):
    return jnp.take_along_axis(table, index, axis=1)


def tile(t):
    return slice(t * LANES, (t + 1) * LANES)


def slab_pick(load, cells, tiles):
    at_lane = cells & (LANES - 1)
    at_tile = lax.shift_right_logical(cells, 7)
    result = jnp.zeros(cells.shape, F32)
    for t in range(tiles):
        result = jnp.where(at_tile == t, lane_pick(load(t), at_lane), result)
    return result


def slab_spread(cell_ref, value_ref, out_ref, tiles):
    fracs = cell_ref.shape[0]

    def body(f, carry):
        cells = cell_ref[pl.ds(f, 1), :]
        value = value_ref[pl.ds(f, 1), :]
        high = value.astype(BF16).astype(F32)
        low = value - high
        at = lax.shift_right_logical(cells, 7) == iota((tiles, LANES), 0)
        left = jnp.concatenate([jnp.where(at, high, 0.0), jnp.where(at, low, 0.0)], 1).astype(BF16)
        hot = jnp.where((cells & (LANES - 1)) == iota((LANES, LANES), 0), 1.0, 0.0).astype(BF16)
        right = jnp.concatenate([hot, hot], 1)
        out_ref[pl.ds(pl.multiple_of(f * tiles, tiles), tiles), :] = mm(left, right, NT)
        return carry

    lax.fori_loop(0, fracs, body, 0, unroll=4)


def cross_hot(rows_at, hot_ref):
    rows, ends = hot_ref.shape
    step = 128

    def body(j, carry):
        base = pl.multiple_of(j * step, step)
        hot_ref[pl.ds(base, step), :] = jnp.where(rows_at == iota((step, ends), 0) + base, 1.0, 0.0).astype(BF16)
        return carry

    lax.fori_loop(0, rows // step, body, 0)


def cross_pick(load, tiles, hot_ref, lane_at):
    table = jnp.concatenate([load(t) for t in range(tiles)], 0)
    high, low = halves(table)
    both = jnp.concatenate([high, low], 1)
    found = mm(both, hot_ref[...], TN)
    found = found[:LANES] + found[LANES:]
    hot = lane_at == iota(found.shape, 0)
    return jnp.sum(jnp.where(hot, found, 0.0), axis=0, keepdims=True)


def cross_spread(values, hot_ref, lane_at, out_ref):
    ends = hot_ref.shape[1]
    hot = lane_at == iota((LANES, ends), 0)
    high = values.astype(BF16).astype(F32)
    low = values - high
    out_ref[...] = mm(hot_ref[...], jnp.where(hot, high, 0.0).astype(BF16), NT) + mm(
        hot_ref[...], jnp.where(hot, low, 0.0).astype(BF16), NT
    )


def ends_swapped(values):
    half = values.shape[1] // 2
    return jnp.concatenate([values[:, half:], values[:, :half]], 1)


def cross_place(pairs_ref, fracs):
    pairs = jnp.concatenate([pairs_ref[0:1, :], pairs_ref[1:2, :]], 1)
    owner = lax.shift_right_logical(pairs, 12)
    row = (lax.shift_right_logical(pairs, 7) & (FSIDE * FSIDE // LANES - 1)) * fracs + owner
    return row, pairs & (LANES - 1)


def frac_setup(
    b_ref, k_ref, st_ref, p_ref, geom_ref, cell_ref, rock_ref, pairs_ref, xgeom_ref, count_ref, offset_ref,
    al_ref, ac_ref, fd_ref, z_ref, cpl_ref, xc_ref, own_ref, up_ref, down_ref, off_ref,
    spread_ref, cross_ref, hot_ref,
):
    fracs, width = b_ref.shape
    tiles = width // LANES
    lane = iota((fracs, LANES), 1)
    row = iota((fracs, LANES), 0)
    inner = (lane & (FSIDE - 1)) < FSIDE - 1
    first = lane < FSIDE

    counts = jnp.zeros((fracs, LANES), jnp.int32)
    offsets = jnp.zeros((fracs, LANES), jnp.int32)
    for f in range(fracs):
        counts = jnp.where(row == f, count_ref[f], counts)
        offsets = jnp.where(row == f, offset_ref[f], offsets)
    off_ref[...] = offsets
    cells = cell_ref[...]
    found = slab_pick(lambda t: p_ref[:, tile(t)], cells, tiles)
    coupling = jnp.where(lane < counts, geom_ref[...] * jnp.exp(-mobility_rate * found), 0.0)
    cpl_ref[...] = coupling
    slab_spread(cell_ref, cpl_ref, spread_ref, tiles)

    rows_at, lane_at = cross_place(pairs_ref, fracs)
    cross_hot(rows_at, hot_ref)
    ends = cross_pick(lambda t: p_ref[:, tile(t)], tiles, hot_ref, lane_at)
    geom = jnp.concatenate([xgeom_ref[...], xgeom_ref[...]], 1)
    xc = geom * jnp.exp(-0.5 * mobility_rate * (ends + ends_swapped(ends)))
    xc_ref[...] = xc
    cross_spread(xc, hot_ref, lane_at, cross_ref)

    def scaled(t):
        k = k_ref[:, tile(t)]
        return k, k * jnp.exp(-0.5 * mobility_rate * p_ref[:, tile(t)])

    k, m = scaled(0)
    k_half, m_half = pltpu.roll(k, FSIDE, 1), pltpu.roll(m, FSIDE, 1)
    before = jnp.zeros((fracs, LANES), F32)
    for t in range(tiles):
        k_one, m_one = pltpu.roll(k, LANES - 1, 1), pltpu.roll(m, LANES - 1, 1)
        along = jnp.where(inner, 2.0 * m * m_one / (k + k_one), 0.0)
        if t + 1 < tiles:
            k_next, m_next = scaled(t + 1)
            k_next_half, m_next_half = pltpu.roll(k_next, FSIDE, 1), pltpu.roll(m_next, FSIDE, 1)
            k_far = jnp.where(first, k_half, k_next_half)
            m_far = jnp.where(first, m_half, m_next_half)
            across = 2.0 * m * m_far / (k + k_far)
        else:
            across = jnp.where(first, 2.0 * m * m_half / (k + k_half), 0.0)
        al_ref[:, tile(t)] = along
        ac_ref[:, tile(t)] = across
        turned = pltpu.roll(across, FSIDE, 1)
        diag = st_ref[:, tile(t)] + along + pltpu.roll(along, 1, 1) + across + jnp.where(first, before, turned)
        diag = diag + spread_ref[pl.ds(t, fracs, stride=tiles), :] + cross_ref[t * fracs : (t + 1) * fracs, :]
        fd_ref[:, tile(t)] = diag
        z_ref[:, tile(t)] = relaxation * b_ref[:, tile(t)] / diag
        before = turned
        if t + 1 < tiles:
            k, m, k_half, m_half = k_next, m_next, k_next_half, m_next_half

    flux = coupling * slab_pick(lambda t: z_ref[:, tile(t)], cells, tiles)
    where_rock = rock_ref[...].astype(F32) + 1.0
    for ref, offset in ((own_ref, 0), (up_ref, 1), (down_ref, -1)):
        ref[0:fracs, :] = jnp.where(offsets == offset, where_rock, 0.0)
        ref[fracs : 2 * fracs, :] = coupling
        ref[2 * fracs : 3 * fracs, :] = flux


def frac_stencil(t, tiles, fd_ref, al_ref, ac_ref, z_ref, first, carry):
    z, z_half, before = carry
    along, across = al_ref[:, tile(t)], ac_ref[:, tile(t)]
    out = fd_ref[:, tile(t)] * z - along * pltpu.roll(z, LANES - 1, 1) - pltpu.roll(along * z, 1, 1)
    turned = pltpu.roll(across * z, FSIDE, 1)
    out = out - jnp.where(first, before, turned)
    if t + 1 < tiles:
        z_next = z_ref[:, tile(t + 1)]
        z_next_half = pltpu.roll(z_next, FSIDE, 1)
        out = out - across * jnp.where(first, z_half, z_next_half)
        return out, (z_next, z_next_half, turned)
    return out - across * z_half, None


def stencil_start(z_ref, fracs):
    z = z_ref[:, tile(0)]
    return z, pltpu.roll(z, FSIDE, 1), jnp.zeros((fracs, LANES), F32)


def sided(parity, even, odd):
    return jnp.where(parity == 0, odd, even), jnp.where(parity == 0, even, odd)


def near_sum(x, v_ref, ylo_ref, yhi_ref, wx_ref, wyp_ref, wym_ref, wzp_ref):
    v = v_ref[x + 1]
    depth = v.shape[0]
    row = iota(v.shape, 0)
    up = jnp.where(row == depth - 1, yhi_ref[pl.ds(x, 1), :], pltpu.roll(v, depth - 1, 0))
    down = jnp.where(row == 0, ylo_ref[pl.ds(x, 1), :], pltpu.roll(v, 1, 0))
    wz = wzp_ref[x]
    total = wx_ref[x + 1] * v_ref[x + 2] + wx_ref[x] * v_ref[x]
    total = total + wyp_ref[x] * up + wym_ref[x] * down
    return v, total + wz * pltpu.roll(v, LANES - 1, 1) + pltpu.roll(wz * v, 1, 1)


def planes(count, body, unroll=4):
    lax.fori_loop(0, count, lambda x, c: (body(x), c)[1], 0, unroll=unroll)


def restrict(values_ref, agg_ref):
    count, depth, _ = values_ref.shape
    block = 16
    sub = iota((8, LANES), 0)
    groups = []
    for base in range(0, NAGG, block):

        def body(x, sums):
            for half in range(depth // 8):
                value = values_ref[x, half * 8 : (half + 1) * 8, :]
                label = agg_ref[x, half * 8 : (half + 1) * 8, :]
                sums = tuple(s + jnp.where(label == base + a, value, 0.0) for a, s in enumerate(sums))
            return sums

        sums = lax.fori_loop(0, count, body, tuple(jnp.zeros((8, LANES), F32) for _ in range(block)), unroll=2)
        for start in range(0, block, 8):
            group = jnp.zeros((8, LANES), F32)
            for a in range(8):
                group = jnp.where(sub == a, jnp.sum(sums[start + a], axis=0, keepdims=True), group)
            groups.append(group)
    groups = groups + [jnp.zeros((8, LANES), F32)] * (LANES // 8 - len(groups))
    table = jnp.concatenate(groups, 0)
    ones = jnp.ones((8, LANES), BF16)
    return sum(mm(ones, part, NT) for part in thirds(table))


def host_cells(cell_ref, g):
    rows = [cell_ref[pl.ds(g * GROUP + i, 1), :] for i in range(GROUP)]
    return jnp.concatenate(rows, 1).astype(jnp.int32) - 1


def host_rows(ref, g):
    return jnp.concatenate([ref[pl.ds(g * GROUP + i, 1), :] for i in range(GROUP)], 1)


def groups_of(count_ref):
    return lax.div(count_ref[0] + GROUP - 1, GROUP)


def host_spread(cell_ref, value_refs, groups, out_ref):
    rows = out_ref.shape[0]
    out_ref[...] = jnp.zeros(out_ref.shape, F32)

    def body(g, carry):
        cells = host_cells(cell_ref, g)
        slots = cells.shape[1]
        at = lax.shift_right_arithmetic(cells, 7)
        left = jnp.where(at == iota((rows, slots), 0), 1.0, 0.0).astype(BF16)
        hot = (cells & (LANES - 1)) == iota((LANES, slots), 0)
        highs, lows = [], []
        for ref in value_refs:
            value = host_rows(ref, g)
            high = value.astype(BF16).astype(F32)
            highs.append(jnp.where(hot, high, 0.0).astype(BF16))
            lows.append(jnp.where(hot, value - high, 0.0).astype(BF16))
        out_ref[...] += mm(left, jnp.concatenate(highs, 0), NT) + mm(left, jnp.concatenate(lows, 0), NT)
        return carry

    lax.fori_loop(0, groups, body, 0)


def host_fetch(table, cell_ref, groups, out_ref):
    rows = table.shape[0]
    high, low = halves(table.T)
    left = jnp.concatenate([high, low], 0)
    out_ref[...] = jnp.zeros(out_ref.shape, F32)

    def body(g, carry):
        cells = host_cells(cell_ref, g)
        slots = cells.shape[1]
        at = lax.shift_right_arithmetic(cells, 7)
        right = jnp.where(at == iota((rows, slots), 0), 1.0, 0.0).astype(BF16)
        found = mm(left, right, (((1,), (0,)), ((), ())))
        found = found[:LANES] + found[LANES:]
        hot = (cells & (LANES - 1)) == iota((LANES, slots), 0)
        value = jnp.sum(jnp.where(hot, found, 0.0), axis=0, keepdims=True)
        for i in range(GROUP):
            out_ref[pl.ds(g * GROUP + i, 1), :] = value[:, i * LANES : (i + 1) * LANES]
        return carry

    lax.fori_loop(0, groups, body, 0)


def reorder(perm, rows):
    return sum(mm(perm, part, (((1,), (0,)), ((), ()))) for part in thirds(rows))


def padded_rows(parts):
    rows = sum(p.shape[0] for p in parts)
    return jnp.concatenate(list(parts) + [jnp.zeros((LANES - rows, LANES), F32)], 0)


def write_layers(parity_x, parity_y, xlo, xhi, ylo, yhi, xe_ref, xo_ref, ye_ref, yo_ref):
    xe_ref[...] = jnp.where(parity_x == 0, xhi, xlo)
    xo_ref[...] = jnp.where(parity_x == 0, xlo, xhi)
    rows = ylo.shape[0]
    ye_ref[0:rows, :] = jnp.where(parity_y == 0, yhi, ylo)
    yo_ref[0:rows, :] = jnp.where(parity_y == 0, ylo, yhi)


def rock_setup(
    b_ref, k_ref, st_ref, p_ref, agg_ref, own_ref, xe_ref, xo_ref, ye_ref, yo_ref, par_ref,
    wx_ref, wyp_ref, wym_ref, wzp_ref, dg_ref, z_ref, flow_ref, cd_ref, cell_ref, perm_ref, unperm_ref, count_ref,
    mxe_ref, mxo_ref, mye_ref, myo_ref,
    kp_ref, mp_ref, kl_ref, kh_ref, ml_ref, mh_ref, cv_ref, fv_ref, grid_ref, cc_ref, ylo_ref, yhi_ref,
):
    nx, ny, _ = b_ref.shape
    fracs = own_ref.shape[0] // 3
    px, py = par_ref[0], par_ref[1]
    rate = -0.5 * mobility_rate

    even, odd = ye_ref[2 * nx :, :], yo_ref[2 * nx :, :]
    below, above = sided(py, even, odd)
    own = own_ref[...]

    def sources(i):
        part = slice(i * fracs, (i + 1) * fracs)
        return padded_rows([own[part], below[part], above[part]])

    cells = sources(0)
    active = jnp.broadcast_to((cells.T)[0:1, :], (8, LANES)) > 0.0
    hot = jnp.where(active, 1.0, 0.0)
    upto = jnp.where(iota((LANES, LANES), 0) <= iota((LANES, LANES), 1), 1.0, 0.0).astype(BF16)
    rank = mm(hot.astype(BF16), upto, (((1,), (0,)), ((), ())))
    place = jnp.where(active, rank, 0.0)[0:1, :].astype(jnp.int32)
    perm = jnp.where(place == iota((LANES, LANES), 0) + 1, 1.0, 0.0)
    perm_ref[...] = perm
    unperm_ref[...] = perm.T
    perm = perm.astype(BF16)
    count_ref[0] = jnp.sum(hot[0:1, :]).astype(jnp.int32)
    cell_ref[...] = reorder(perm, cells)
    cv_ref[...] = reorder(perm, sources(1))
    fv_ref[...] = reorder(perm, sources(2))
    host_spread(cell_ref, (cv_ref, fv_ref), groups_of(count_ref), grid_ref)

    k_lo, k_hi = sided(px, xe_ref[0:ny, :], xo_ref[0:ny, :])
    p_lo, p_hi = sided(px, xe_ref[ny : 2 * ny, :], xo_ref[ny : 2 * ny, :])
    kp_ref[0] = k_lo
    kp_ref[nx + 1] = k_hi
    mp_ref[0] = k_lo * jnp.exp(rate * p_lo)
    mp_ref[nx + 1] = k_hi * jnp.exp(rate * p_hi)
    k_lo, k_hi = sided(py, ye_ref[0:nx, :], yo_ref[0:nx, :])
    p_lo, p_hi = sided(py, ye_ref[nx : 2 * nx, :], yo_ref[nx : 2 * nx, :])
    kl_ref[...] = k_lo
    kh_ref[...] = k_hi
    ml_ref[...] = k_lo * jnp.exp(rate * p_lo)
    mh_ref[...] = k_hi * jnp.exp(rate * p_hi)

    def scale(x):
        k = k_ref[x]
        kp_ref[x + 1] = k
        mp_ref[x + 1] = k * jnp.exp(rate * p_ref[x])

    planes(nx, scale)
    row = iota((ny, LANES), 0)
    lane = iota((ny, LANES), 1)

    def face_x(x):
        wx_ref[x] = 2.0 * mp_ref[x] * mp_ref[x + 1] / (kp_ref[x] + kp_ref[x + 1])

    planes(nx + 1, face_x, unroll=3)

    def assemble(x):
        k, m = kp_ref[x + 1], mp_ref[x + 1]
        k_up = jnp.where(row == ny - 1, kh_ref[pl.ds(x, 1), :], pltpu.roll(k, ny - 1, 0))
        m_up = jnp.where(row == ny - 1, mh_ref[pl.ds(x, 1), :], pltpu.roll(m, ny - 1, 0))
        wyp = 2.0 * m * m_up / (k + k_up)
        edge = 2.0 * m * ml_ref[pl.ds(x, 1), :] / (k + kl_ref[pl.ds(x, 1), :])
        wym = jnp.where(row == 0, edge, pltpu.roll(wyp, 1, 0))
        wzp = 2.0 * m * pltpu.roll(m, LANES - 1, 1) / (k + pltpu.roll(k, LANES - 1, 1))
        wzp = jnp.where(lane < LANES - 1, wzp, 0.0)
        wzm = pltpu.roll(wzp, 1, 1)
        wyp_ref[x] = wyp
        wym_ref[x] = wym
        wzp_ref[x] = wzp
        at = pl.ds(pl.multiple_of(x * ny, ny), ny)
        base = st_ref[x] + grid_ref[at, 0:LANES]
        flow_ref[x] = grid_ref[at, LANES:]
        wxm, wxp = wx_ref[x], wx_ref[x + 1]
        diag = base + wxm + wxp + wyp + wym + wzp + wzm
        dg_ref[x] = diag
        z = relaxation * b_ref[x] / diag
        z_ref[x] = z
        ylo_ref[pl.ds(x, 1), :] = z[0:1, :]
        yhi_ref[pl.ds(x, 1), :] = z[ny - 1 : ny, :]
        label = agg_ref[x]
        coarse = base + jnp.where((x > 0) & (agg_ref[jnp.maximum(x - 1, 0)] == label), 0.0, wxm)
        coarse = coarse + jnp.where((x < nx - 1) & (agg_ref[jnp.minimum(x + 1, nx - 1)] == label), 0.0, wxp)
        coarse = coarse + jnp.where((row < ny - 1) & (pltpu.roll(label, ny - 1, 0) == label), 0.0, wyp)
        coarse = coarse + jnp.where((row > 0) & (pltpu.roll(label, 1, 0) == label), 0.0, wym)
        coarse = coarse + jnp.where(pltpu.roll(label, LANES - 1, 1) == label, 0.0, wzp)
        coarse = coarse + jnp.where(pltpu.roll(label, 1, 1) == label, 0.0, wzm)
        cc_ref[x] = coarse

    planes(nx, assemble, unroll=2)
    sums = restrict(cc_ref, agg_ref)
    cd_ref[...] = jnp.where(iota((8, LANES), 1) < NAGG, sums, 1.0)
    write_layers(
        px, py, z_ref[0], z_ref[nx - 1], ylo_ref[...], yhi_ref[...], mxe_ref, mxo_ref, mye_ref, myo_ref
    )


def fill_halo(vp_ref, v_ref, ylo_ref, yhi_ref, px, py, xe_ref, xo_ref, ye_ref, yo_ref):
    nx, ny, _ = v_ref.shape
    low, high = sided(px, xe_ref[...], xo_ref[...])
    vp_ref[0] = low
    vp_ref[nx + 1] = high

    def copy(x):
        vp_ref[x + 1] = v_ref[x]

    planes(nx, copy)
    low, high = sided(py, ye_ref[0:nx, :], yo_ref[0:nx, :])
    ylo_ref[...] = low
    yhi_ref[...] = high


def coarse_step(
    first, px, py, r_ref, z_ref, flow_of, agg_ref, weights, dg_ref, cd_ref, cell_ref, unperm_ref, count_ref,
    p_ref, hv_ref, messages, vp_ref, ylo_ref, yhi_ref, s_ref, hc_ref,
):
    nx, ny, _ = z_ref.shape
    fracs = hv_ref.shape[0]

    def residual(x):
        v, near = near_sum(x, vp_ref, ylo_ref, yhi_ref, *weights)
        s_ref[x] = (1.0 - relaxation) * r_ref[x] + near + flow_of(x)

    planes(nx, residual)
    solved = restrict(s_ref, agg_ref) / cd_ref[...]

    def correct(x):
        z = vp_ref[x + 1]
        label = agg_ref[x]
        parts = [lane_pick(solved, label[h * 8 : (h + 1) * 8, :]) for h in range(ny // 8)]
        p = z + jnp.concatenate(parts, 0)
        p_ref[x] = p
        s_ref[x] = p
        ylo_ref[pl.ds(x, 1), :] = p[0:1, :]
        yhi_ref[pl.ds(x, 1), :] = p[ny - 1 : ny, :]

    planes(nx, correct)
    table = s_ref[...].reshape(nx * ny, LANES)
    host_fetch(table, cell_ref, groups_of(count_ref), hc_ref)
    values = reorder(unperm_ref[...].astype(BF16), hc_ref[...])
    hv_ref[...] = values[0:fracs]
    below, above = values[fracs : 2 * fracs], values[2 * fracs : 3 * fracs]
    write_layers(px, py, s_ref[0], s_ref[nx - 1], ylo_ref[...], yhi_ref[...], *messages)
    ye_ref, yo_ref = messages[2], messages[3]
    ye_ref[nx:, :] = jnp.where(py == 0, above, below)
    yo_ref[nx:, :] = jnp.where(py == 0, below, above)


def precond_first(
    b_ref, z_ref, flow_ref, agg_ref, wx_ref, wyp_ref, wym_ref, wzp_ref, dg_ref, cd_ref, cell_ref, unperm_ref,
    xe_ref, xo_ref, ye_ref, yo_ref, par_ref, count_ref,
    p_ref, hv_ref, mxe_ref, mxo_ref, mye_ref, myo_ref,
    vp_ref, ylo_ref, yhi_ref, s_ref, hc_ref,
):
    px, py = par_ref[0], par_ref[1]
    fill_halo(vp_ref, z_ref, ylo_ref, yhi_ref, px, py, xe_ref, xo_ref, ye_ref, yo_ref)
    coarse_step(
        True, px, py, b_ref, z_ref, lambda x: flow_ref[x], agg_ref, (wx_ref, wyp_ref, wym_ref, wzp_ref),
        dg_ref, cd_ref, cell_ref, unperm_ref, count_ref, p_ref, hv_ref, (mxe_ref, mxo_ref, mye_ref, myo_ref),
        vp_ref, ylo_ref, yhi_ref, s_ref, hc_ref,
    )


def hosted_values(hv_ref, off_ref, py, ye_ref, yo_ref, nx):
    below, above = sided(py, ye_ref[nx:, :], yo_ref[nx:, :])
    offsets = off_ref[...]
    return jnp.where(offsets == 0, hv_ref[...], jnp.where(offsets == 1, above, below))


def image_first(
    p_ref, flow_ref, wx_ref, wyp_ref, wym_ref, wzp_ref, dg_ref, hv_ref, off_ref,
    fd_ref, al_ref, ac_ref, zf_ref, cpl_ref, cell_ref, xc_ref, pairs_ref, xe_ref, xo_ref, ye_ref, yo_ref, par_ref,
    u_ref, z_ref, uf_ref, zn_ref, flux_ref, mxe_ref, mxo_ref, mye_ref, myo_ref,
    vp_ref, ylo_ref, yhi_ref, slot_ref, spread_ref, cross_ref, hot_ref,
):
    nx, ny, _ = p_ref.shape
    fracs, width = zf_ref.shape
    tiles = width // LANES
    px, py = par_ref[0], par_ref[1]
    fill_halo(vp_ref, p_ref, ylo_ref, yhi_ref, px, py, xe_ref, xo_ref, ye_ref, yo_ref)
    weights = (wx_ref, wyp_ref, wym_ref, wzp_ref)

    def image(x):
        v, near = near_sum(x, vp_ref, ylo_ref, yhi_ref, *weights)
        diag = dg_ref[x]
        u = diag * v - near - flow_ref[x]
        u_ref[x] = u
        z_ref[x] = relaxation * u / diag

    planes(nx, image)

    slot_ref[...] = cpl_ref[...] * hosted_values(hv_ref, off_ref, py, ye_ref, yo_ref, nx)
    slab_spread(cell_ref, slot_ref, spread_ref, tiles)
    rows_at, lane_at = cross_place(pairs_ref, fracs)
    cross_hot(rows_at, hot_ref)
    ends = cross_pick(lambda t: zf_ref[:, tile(t)], tiles, hot_ref, lane_at)
    cross_spread(xc_ref[...] * ends_swapped(ends), hot_ref, lane_at, cross_ref)
    first = iota((fracs, LANES), 1) < FSIDE
    carry = stencil_start(zf_ref, fracs)
    for t in range(tiles):
        out, carry = frac_stencil(t, tiles, fd_ref, al_ref, ac_ref, zf_ref, first, carry)
        out = out - spread_ref[pl.ds(t, fracs, stride=tiles), :] - cross_ref[t * fracs : (t + 1) * fracs, :]
        uf_ref[:, tile(t)] = out
        zn_ref[:, tile(t)] = relaxation * out / fd_ref[:, tile(t)]
    flux = cpl_ref[...] * slab_pick(lambda t: zn_ref[:, tile(t)], cell_ref[...], tiles)
    flux_ref[...] = flux

    for x in range(nx):
        ylo_ref[x : x + 1, :] = z_ref[x, 0:1, :]
        yhi_ref[x : x + 1, :] = z_ref[x, ny - 1 : ny, :]
    write_layers(
        px, py, z_ref[0], z_ref[nx - 1], ylo_ref[...], yhi_ref[...], mxe_ref, mxo_ref, mye_ref, myo_ref
    )
    mye_ref[nx:, :] = flux
    myo_ref[nx:, :] = flux


def precond_second(
    u_ref, z_ref, flux_ref, agg_ref, wx_ref, wyp_ref, wym_ref, wzp_ref, dg_ref, cd_ref, cell_ref, perm_ref, unperm_ref,
    xe_ref, xo_ref, ye_ref, yo_ref, par_ref, count_ref,
    p_ref, hv_ref, flow_ref, mxe_ref, mxo_ref, mye_ref, myo_ref,
    vp_ref, ylo_ref, yhi_ref, s_ref, hc_ref, fv_ref, grid_ref,
):
    nx, ny, _ = z_ref.shape
    px, py = par_ref[0], par_ref[1]
    fill_halo(vp_ref, z_ref, ylo_ref, yhi_ref, px, py, xe_ref, xo_ref, ye_ref, yo_ref)
    below, above = sided(py, ye_ref[nx:, :], yo_ref[nx:, :])
    fv_ref[...] = reorder(perm_ref[...].astype(BF16), padded_rows([flux_ref[...], below, above]))
    host_spread(cell_ref, (fv_ref,), groups_of(count_ref), grid_ref)

    def flow_of(x):
        flow = grid_ref[pl.ds(pl.multiple_of(x * ny, ny), ny), :]
        flow_ref[x] = flow
        return flow

    coarse_step(
        False, px, py, u_ref, z_ref, flow_of, agg_ref, (wx_ref, wyp_ref, wym_ref, wzp_ref),
        dg_ref, cd_ref, cell_ref, unperm_ref, count_ref, p_ref, hv_ref, (mxe_ref, mxo_ref, mye_ref, myo_ref),
        vp_ref, ylo_ref, yhi_ref, s_ref, hc_ref,
    )


def frac_second(
    fd_ref, al_ref, ac_ref, z_ref, xc_ref, pairs_ref,
    q_ref,
    cross_ref, hot_ref,
):
    fracs, width = z_ref.shape
    tiles = width // LANES
    rows_at, lane_at = cross_place(pairs_ref, fracs)
    cross_hot(rows_at, hot_ref)
    ends = cross_pick(lambda t: z_ref[:, tile(t)], tiles, hot_ref, lane_at)
    cross_spread(xc_ref[...] * ends_swapped(ends), hot_ref, lane_at, cross_ref)
    first = iota((fracs, LANES), 1) < FSIDE
    carry = stencil_start(z_ref, fracs)
    for t in range(tiles):
        out, carry = frac_stencil(t, tiles, fd_ref, al_ref, ac_ref, z_ref, first, carry)
        q_ref[:, tile(t)] = out - cross_ref[t * fracs : (t + 1) * fracs, :]


def products(b, u, w):
    return (b * b, u * b, u * u, w * b, w * u, w * w)


def image_second(
    p_ref, flow_ref, wx_ref, wyp_ref, wym_ref, wzp_ref, dg_ref, b_ref, u_ref, hv_ref, off_ref,
    q_ref, cpl_ref, cell_ref, bf_ref, uf_ref, xe_ref, xo_ref, ye_ref, yo_ref, par_ref,
    sums_ref,
    vp_ref, ylo_ref, yhi_ref, slot_ref, spread_ref,
):
    nx, ny, _ = p_ref.shape
    fracs, width = q_ref.shape
    tiles = width // LANES
    px, py = par_ref[0], par_ref[1]
    fill_halo(vp_ref, p_ref, ylo_ref, yhi_ref, px, py, xe_ref, xo_ref, ye_ref, yo_ref)
    weights = (wx_ref, wyp_ref, wym_ref, wzp_ref)

    def image(x, sums):
        v, near = near_sum(x, vp_ref, ylo_ref, yhi_ref, *weights)
        w = dg_ref[x] * v - near - flow_ref[x]
        return tuple(s + t for s, t in zip(sums, products(b_ref[x], u_ref[x], w)))

    rock = lax.fori_loop(0, nx, image, tuple(jnp.zeros((ny, LANES), F32) for _ in range(6)), unroll=4)
    slot_ref[...] = cpl_ref[...] * hosted_values(hv_ref, off_ref, py, ye_ref, yo_ref, nx)
    slab_spread(cell_ref, slot_ref, spread_ref, tiles)
    frac = [jnp.zeros((fracs, LANES), F32) for _ in range(6)]
    for t in range(tiles):
        w = q_ref[:, tile(t)] - spread_ref[pl.ds(t, fracs, stride=tiles), :]
        frac = [s + t_ for s, t_ in zip(frac, products(bf_ref[:, tile(t)], uf_ref[:, tile(t)], w))]
    sub = iota((8, LANES), 0)
    table = jnp.zeros((8, LANES), F32)
    for i in range(6):
        total = jnp.sum(rock[i], axis=0, keepdims=True) + jnp.sum(frac[i], axis=0, keepdims=True)
        table = jnp.where(sub == i, total, table)
    table = jnp.concatenate([table, jnp.zeros((LANES - 8, LANES), F32)], 0)
    ones = jnp.ones((8, LANES), BF16)
    row = sum(mm(ones, part, NT) for part in thirds(table))[0:1, :]
    sums_ref[...] = jnp.broadcast_to(row, sums_ref.shape)


def finish(all_ref, p_ref, q_ref, pf_ref, qf_ref, rock_ref, frac_ref, res_ref):
    total = jnp.sum(all_ref[...], axis=0, keepdims=True)
    total = jnp.broadcast_to(total, (8, LANES))
    bb, ub, uu, wb, wu, ww = (
        lane_pick(total, jnp.full((8, LANES), i, jnp.int32)) for i in range(6)
    )
    norm2 = bb + epsilon
    norm = jnp.sqrt(norm2)
    h00 = ub / norm2
    n1 = jnp.maximum(uu - 2.0 * h00 * ub + h00 * h00 * bb, 0.0) / norm2
    h10 = jnp.sqrt(n1 + epsilon)
    h01 = (wb - h00 * ub) / (norm2 * h10)
    h11 = (wu - h00 * wb - h00 * uu + h00 * h00 * ub) / (norm2 * h10 * h10)
    square = (ww - 2.0 * h00 * wu + h00 * h00 * uu) / (norm2 * h10 * h10)
    v00 = bb / norm2
    v11 = n1 / (h10 * h10)
    v01 = (ub - h00 * bb) / (norm2 * h10)
    n2 = square + h01 * h01 * (v00 - 2.0) + h11 * h11 * (v11 - 2.0) + 2.0 * h01 * h11 * v01
    h21 = jnp.sqrt(jnp.maximum(n2, epsilon * square) + epsilon)
    r0 = jnp.sqrt(h00 * h00 + h10 * h10)
    c0, s0 = h00 / r0, h10 / r0
    top = c0 * h01 + s0 * h11
    low = c0 * h11 - s0 * h01
    r1 = jnp.sqrt(low * low + h21 * h21)
    c1, s1 = low / r1, h21 / r1
    g0, g1 = c0 * norm, -s0 * norm
    y1 = c1 * g1 / r1
    y0 = (g0 - top * y1) / r0
    residual = jnp.abs(s1 * g1)
    beta = y1 / (norm * h10)
    alpha = y0 / norm - h00 * beta
    res_ref[0, 0] = residual[0, 0]
    nx, ny, _ = p_ref.shape
    alpha_y, beta_y = alpha[0:1, :], beta[0:1, :]

    def rock(x):
        rock_ref[x] = alpha_y * p_ref[x] + beta_y * q_ref[x]

    planes(nx, rock)
    for t in range(pf_ref.shape[1] // LANES):
        frac_ref[:, tile(t)] = alpha_y * pf_ref[:, tile(t)] + beta_y * qf_ref[:, tile(t)]


def local(
    rock_rhs,
    frac_rhs,
    perm,
    storage,
    pressure,
    frac_perm,
    frac_storage,
    frac_pressure,
    couple_geom,
    couple_count,
    couple_frac_cell,
    couple_rock_cell,
    host_offset,
    cross_pairs,
    cross_geom,
    aggregates,
):
    nx, ny, nz = rock_rhs.shape
    fracs, width = frac_rhs.shape
    pairs = cross_pairs.shape[1]
    tiles = width // LANES
    cube, slab, slots = shaped(nx, ny, nz), shaped(fracs, width), shaped(fracs, LANES)
    gx, gy = lax.axis_index("gx"), lax.axis_index("gy")
    parity = jnp.stack([gx % 2, gy % 2]).astype(jnp.int32)
    vcube = pltpu.VMEM((nx, ny, nz), F32)
    vpad = pltpu.VMEM((nx + 2, ny, nz), F32)
    vside = pltpu.VMEM((nx, nz), F32)
    vhost = pltpu.VMEM((LANES, LANES), F32)
    vcross = pltpu.VMEM((fracs * tiles, LANES), F32)
    vhot = pltpu.VMEM((fracs * tiles, 2 * pairs), BF16)
    vslots = pltpu.VMEM((fracs, LANES), F32)

    even_x, even_y = gx % 2 == 0, gy % 2 == 0
    stacked = (perm, pressure)
    x_lo = jnp.concatenate([a[0] for a in stacked], 0)
    x_hi = jnp.concatenate([a[nx - 1] for a in stacked], 0)
    y_lo = jnp.concatenate([a[:, 0] for a in stacked], 0)
    y_hi = jnp.concatenate([a[:, ny - 1] for a in stacked], 0)
    x_even, x_odd = exchange(jnp.where(even_x, x_hi, x_lo), jnp.where(even_x, x_lo, x_hi), "gx")

    al, ac, fd, zf, cpl, xc, own, up, down, off = call(
        frac_setup,
        [slab, slab, slab, slab, slots, shaped(1, 2 * pairs)]
        + [shaped(3 * fracs, LANES)] * 3
        + [shaped(fracs, LANES, dtype=jnp.int32)],
        [
            frac_rhs, frac_perm, frac_storage, frac_pressure, couple_geom, couple_frac_cell, couple_rock_cell,
            cross_pairs, cross_geom.reshape(1, pairs), couple_count, host_offset,
        ],
        [vcross, vcross, vhot],
        smem_in=(9, 10),
    )
    to_even = jnp.where(even_y, jnp.concatenate([y_hi, up], 0), jnp.concatenate([y_lo, down], 0))
    to_odd = jnp.where(even_y, jnp.concatenate([y_lo, down], 0), jnp.concatenate([y_hi, up], 0))
    y_even, y_odd = exchange(to_even, to_odd, "gy")

    layers = [shaped(ny, nz), shaped(ny, nz)]
    count_shape = shaped(1, dtype=jnp.int32)
    host_shape = shaped(LANES, LANES)
    wx, wyp, wym, wzp, dg, z0, flow0, cd, cells, pack, unpack, count, xe, xo, ye, yo = call(
        rock_setup,
        [shaped(nx + 1, ny, nz), cube, cube, cube, cube, cube, cube, shaped(8, LANES)]
        + [host_shape] * 3
        + [count_shape]
        + layers
        + [shaped(nx, nz)] * 2,
        [rock_rhs, perm, storage, pressure, aggregates, own, x_even, x_odd, y_even, y_odd, parity],
        [vpad, vpad, vside, vside, vside, vside, vhost, vhost, pltpu.VMEM((nx * ny, 2 * LANES), F32), vcube, vside, vside],
        smem_in=(10,),
        smem_out=(11,),
    )
    weights = [wx, wyp, wym, wzp]
    xe, xo = exchange(xe, xo, "gx")
    ye, yo = exchange(ye, yo, "gy")
    p0, hv, xe, xo, ye, yo = call(
        precond_first,
        [cube, slots] + layers + [shaped(nx + fracs, nz)] * 2,
        [rock_rhs, z0, flow0, aggregates] + weights + [dg, cd, cells, unpack, xe, xo, ye, yo, parity, count],
        [vpad, vside, vside, vcube, vhost],
        smem_in=(16, 17),
    )
    xe, xo = exchange(xe, xo, "gx")
    ye, yo = exchange(ye, yo, "gy")
    u0, z1, uf0, zf1, flux1, xe, xo, ye, yo = call(
        image_first,
        [cube, cube, slab, slab, slots] + layers + [shaped(nx + fracs, nz)] * 2,
        [p0, flow0] + weights + [dg, hv, off, fd, al, ac, zf, cpl, couple_frac_cell, xc, cross_pairs, xe, xo, ye, yo, parity],
        [vpad, vside, vside, vslots, vcross, vcross, vhot],
        smem_in=(21,),
    )
    xe, xo = exchange(xe, xo, "gx")
    ye, yo = exchange(ye, yo, "gy")
    p1, hv, flow1, xe, xo, ye, yo = call(
        precond_second,
        [cube, slots, cube] + layers + [shaped(nx + fracs, nz)] * 2,
        [u0, z1, flux1, aggregates] + weights + [dg, cd, cells, pack, unpack, xe, xo, ye, yo, parity, count],
        [vpad, vside, vside, vcube, vhost, vhost, pltpu.VMEM((nx * ny, LANES), F32)],
        smem_in=(17, 18),
    )
    xe, xo = exchange(xe, xo, "gx")
    ye, yo = exchange(ye, yo, "gy")
    (q1,) = call(
        frac_second, [slab], [fd, al, ac, zf1, xc, cross_pairs], [vcross, vhot]
    )
    devices = lax.axis_size("gx") * lax.axis_size("gy")
    (sums,) = call(
        image_second,
        [shaped(devices, LANES)],
        [p1, flow1] + weights + [dg, rock_rhs, u0, hv, off, q1, cpl, couple_frac_cell, frac_rhs, uf0, xe, xo, ye, yo, parity],
        [vpad, vside, vside, vslots, vcross],
        smem_in=(20,),
    )
    gathered = lax.all_to_all(sums, ("gx", "gy"), 0, 0, tiled=True)
    rock_update, frac_update, residual = call(
        finish,
        [cube, slab, shaped(1, 1)],
        [gathered, p0, p1, zf, zf1],
        smem_out=(2,),
    )
    return rock_update, frac_update, residual.reshape(())


def solution(mesh):
    placed = (
        P("gx", "gy", None),
        P(("gx", "gy"), None),
        P("gx", "gy", None),
        P("gx", "gy", None),
        P("gx", "gy", None),
        P(("gx", "gy"), None),
        P(("gx", "gy"), None),
        P(("gx", "gy"), None),
        P(("gx", "gy"), None),
        P(("gx", "gy")),
        P(("gx", "gy"), None),
        P(("gx", "gy"), None),
        P(("gx", "gy")),
        P(None, ("gx", "gy")),
        P(("gx", "gy")),
        P("gx", "gy", None),
    )
    return jax.shard_map(
        local,
        mesh=mesh,
        in_specs=placed,
        out_specs=(P("gx", "gy", None), P(("gx", "gy"), None), P()),
        check_vma=False,
    )
```

```python
import functools

import jax
import jax.numpy as jnp
from jax import lax
from jax.experimental import pallas as pl
from jax.experimental.pallas import tpu as pltpu
from jax.sharding import PartitionSpec as P

FSIDE = 64
NAGG = 64
LANES = 128
GROUP = 4
CHUNK = 8

mobility_rate = 0.5
relaxation = 0.8
epsilon = 1e-06
F32 = jnp.float32
BF16 = jnp.bfloat16
NT = (((1,), (1,)), ((), ()))
TN = (((0,), (0,)), ((), ()))
VM = pl.BlockSpec(memory_space=pltpu.VMEM)
SM = pl.BlockSpec(memory_space=pltpu.SMEM)
HB = pl.BlockSpec(memory_space=pltpu.HBM)


def call(kernel, outs, ins, scratch=(), flops=1 << 24, smem_in=(), smem_out=(), hbm_in=(), limit=24):
    nbytes = sum(a.size * a.dtype.itemsize for a in list(ins) + list(outs))
    return pl.pallas_call(
        kernel,
        out_shape=tuple(outs),
        in_specs=[SM if i in smem_in else HB if i in hbm_in else VM for i in range(len(ins))],
        out_specs=tuple(SM if i in smem_out else VM for i in range(len(outs))),
        scratch_shapes=list(scratch),
        cost_estimate=pl.CostEstimate(flops=flops, bytes_accessed=nbytes, transcendentals=0),
        compiler_params=pltpu.CompilerParams(vmem_limit_bytes=limit << 20),
    )(*ins)


def shaped(*dims, dtype=F32):
    return jax.ShapeDtypeStruct(dims, dtype)


def swap_pairs(n):
    even = [(i, i ^ 1) for i in range(n) if i ^ 1 < n]
    odd = [(i, ((i - 1) ^ 1) + 1) for i in range(1, n) if ((i - 1) ^ 1) + 1 < n]
    return even, odd


def exchange(even_msg, odd_msg, axis):
    even, odd = swap_pairs(lax.axis_size(axis))
    return lax.ppermute(even_msg, axis, even), lax.ppermute(odd_msg, axis, odd)


def halves(value):
    high = value.astype(BF16)
    return high, (value - high.astype(F32)).astype(BF16)


def thirds(value):
    high = value.astype(BF16)
    rest = value - high.astype(F32)
    mid = rest.astype(BF16)
    return high, mid, (rest - mid.astype(F32)).astype(BF16)


def mm(lhs, rhs, dims):
    return lax.dot_general(lhs, rhs, dims, preferred_element_type=F32)


def iota(shape, dim):
    return lax.broadcasted_iota(jnp.int32, shape, dim)


def lane_pick(table, index):
    return jnp.take_along_axis(table, index, axis=1)


def tile(t):
    return slice(t * LANES, (t + 1) * LANES)


def slab_pick(load, cells, tiles):
    at_lane = cells & (LANES - 1)
    at_tile = lax.shift_right_logical(cells, 7)
    result = jnp.zeros(cells.shape, F32)
    for t in range(tiles):
        result = jnp.where(at_tile == t, lane_pick(load(t), at_lane), result)
    return result


def slab_spread(cell_ref, value_ref, out_ref, tiles):
    fracs = cell_ref.shape[0]

    def body(f, carry):
        cells = cell_ref[pl.ds(f, 1), :]
        value = value_ref[pl.ds(f, 1), :]
        high = value.astype(BF16).astype(F32)
        low = value - high
        at = lax.shift_right_logical(cells, 7) == iota((tiles, LANES), 0)
        left = jnp.concatenate([jnp.where(at, high, 0.0), jnp.where(at, low, 0.0)], 1).astype(BF16)
        hot = jnp.where((cells & (LANES - 1)) == iota((LANES, LANES), 0), 1.0, 0.0).astype(BF16)
        right = jnp.concatenate([hot, hot], 1)
        out_ref[pl.ds(pl.multiple_of(f * tiles, tiles), tiles), :] = mm(left, right, NT)
        return carry

    lax.fori_loop(0, fracs, body, 0, unroll=4)


def cross_hot(rows_at, hot_ref):
    rows, ends = hot_ref.shape
    step = 128

    def body(j, carry):
        base = pl.multiple_of(j * step, step)
        hot_ref[pl.ds(base, step), :] = jnp.where(rows_at == iota((step, ends), 0) + base, 1.0, 0.0).astype(BF16)
        return carry

    lax.fori_loop(0, rows // step, body, 0)


def cross_pick(load, tiles, hot_ref, lane_at):
    table = jnp.concatenate([load(t) for t in range(tiles)], 0)
    high, low = halves(table)
    both = jnp.concatenate([high, low], 1)
    found = mm(both, hot_ref[...], TN)
    found = found[:LANES] + found[LANES:]
    hot = lane_at == iota(found.shape, 0)
    return jnp.sum(jnp.where(hot, found, 0.0), axis=0, keepdims=True)


def cross_spread(values, hot_ref, lane_at, out_ref):
    ends = hot_ref.shape[1]
    hot = lane_at == iota((LANES, ends), 0)
    high = values.astype(BF16).astype(F32)
    low = values - high
    out_ref[...] = mm(hot_ref[...], jnp.where(hot, high, 0.0).astype(BF16), NT) + mm(
        hot_ref[...], jnp.where(hot, low, 0.0).astype(BF16), NT
    )


def ends_swapped(values):
    half = values.shape[1] // 2
    return jnp.concatenate([values[:, half:], values[:, :half]], 1)


def cross_place(pairs_ref, fracs):
    pairs = jnp.concatenate([pairs_ref[0:1, :], pairs_ref[1:2, :]], 1)
    owner = lax.shift_right_logical(pairs, 12)
    row = (lax.shift_right_logical(pairs, 7) & (FSIDE * FSIDE // LANES - 1)) * fracs + owner
    return row, pairs & (LANES - 1)


def frac_setup(
    b_ref, k_ref, st_ref, p_ref, geom_ref, cell_ref, rock_ref, pairs_ref, xgeom_ref, count_ref, offset_ref,
    perm_hbm, press_hbm, par_ref,
    al_ref, ac_ref, fd_ref, z_ref, cpl_ref, xc_ref, own_ref, even_ref, odd_ref, off_ref,
    spread_ref, cross_ref, hot_ref, side_ref, sems,
):
    last = perm_hbm.shape[1] - 1
    copies = [
        pltpu.make_async_copy(source, target, sems.at[i])
        for i, (source, target) in enumerate(
            [
                (perm_hbm.at[:, 0, :], side_ref.at[0]),
                (press_hbm.at[:, 0, :], side_ref.at[1]),
                (perm_hbm.at[:, last, :], side_ref.at[2]),
                (press_hbm.at[:, last, :], side_ref.at[3]),
            ]
        )
    ]
    for copy in copies:
        copy.start()
    fracs, width = b_ref.shape
    tiles = width // LANES
    lane = iota((fracs, LANES), 1)
    row = iota((fracs, LANES), 0)
    inner = (lane & (FSIDE - 1)) < FSIDE - 1
    first = lane < FSIDE

    counts = jnp.zeros((fracs, LANES), jnp.int32)
    offsets = jnp.zeros((fracs, LANES), jnp.int32)
    for f in range(fracs):
        counts = jnp.where(row == f, count_ref[f], counts)
        offsets = jnp.where(row == f, offset_ref[f], offsets)
    off_ref[...] = offsets
    cells = cell_ref[...]
    found = slab_pick(lambda t: p_ref[:, tile(t)], cells, tiles)
    coupling = jnp.where(lane < counts, geom_ref[...] * jnp.exp(-mobility_rate * found), 0.0)
    cpl_ref[...] = coupling
    slab_spread(cell_ref, cpl_ref, spread_ref, tiles)

    rows_at, lane_at = cross_place(pairs_ref, fracs)
    cross_hot(rows_at, hot_ref)
    ends = cross_pick(lambda t: p_ref[:, tile(t)], tiles, hot_ref, lane_at)
    geom = jnp.concatenate([xgeom_ref[...], xgeom_ref[...]], 1)
    xc = geom * jnp.exp(-0.5 * mobility_rate * (ends + ends_swapped(ends)))
    xc_ref[...] = xc
    cross_spread(xc, hot_ref, lane_at, cross_ref)

    def scaled(t):
        k = k_ref[:, tile(t)]
        return k, k * jnp.exp(-0.5 * mobility_rate * p_ref[:, tile(t)])

    k, m = scaled(0)
    k_half, m_half = pltpu.roll(k, FSIDE, 1), pltpu.roll(m, FSIDE, 1)
    before = jnp.zeros((fracs, LANES), F32)
    for t in range(tiles):
        k_one, m_one = pltpu.roll(k, LANES - 1, 1), pltpu.roll(m, LANES - 1, 1)
        along = jnp.where(inner, 2.0 * m * m_one / (k + k_one), 0.0)
        if t + 1 < tiles:
            k_next, m_next = scaled(t + 1)
            k_next_half, m_next_half = pltpu.roll(k_next, FSIDE, 1), pltpu.roll(m_next, FSIDE, 1)
            k_far = jnp.where(first, k_half, k_next_half)
            m_far = jnp.where(first, m_half, m_next_half)
            across = 2.0 * m * m_far / (k + k_far)
        else:
            across = jnp.where(first, 2.0 * m * m_half / (k + k_half), 0.0)
        al_ref[:, tile(t)] = along
        ac_ref[:, tile(t)] = across
        turned = pltpu.roll(across, FSIDE, 1)
        diag = st_ref[:, tile(t)] + along + pltpu.roll(along, 1, 1) + across + jnp.where(first, before, turned)
        diag = diag + spread_ref[pl.ds(t, fracs, stride=tiles), :] + cross_ref[t * fracs : (t + 1) * fracs, :]
        fd_ref[:, tile(t)] = diag
        z_ref[:, tile(t)] = relaxation * b_ref[:, tile(t)] / diag
        before = turned
        if t + 1 < tiles:
            k, m, k_half, m_half = k_next, m_next, k_next_half, m_next_half

    flux = coupling * slab_pick(lambda t: z_ref[:, tile(t)], cells, tiles)
    where_rock = rock_ref[...].astype(F32) + 1.0
    own_ref[0:fracs, :] = jnp.where(offsets == 0, where_rock, 0.0)
    own_ref[fracs : 2 * fracs, :] = coupling
    own_ref[2 * fracs : 3 * fracs, :] = flux
    for copy in copies:
        copy.wait()
    sides = side_ref.shape[1]
    even_up = par_ref[1] == 0
    for ref, up in ((even_ref, even_up), (odd_ref, jnp.logical_not(even_up))):
        ref[0:sides, :] = jnp.where(up, side_ref[2], side_ref[0])
        ref[sides : 2 * sides, :] = jnp.where(up, side_ref[3], side_ref[1])
        rest = ref.at[2 * sides :, :]
        rest[0:fracs, :] = jnp.where(offsets == jnp.where(up, 1, -1), where_rock, 0.0)
        rest[fracs : 2 * fracs, :] = coupling
        rest[2 * fracs : 3 * fracs, :] = flux


def frac_stencil(t, tiles, fd_ref, al_ref, ac_ref, z_ref, first, carry):
    z, z_half, before = carry
    along, across = al_ref[:, tile(t)], ac_ref[:, tile(t)]
    out = fd_ref[:, tile(t)] * z - along * pltpu.roll(z, LANES - 1, 1) - pltpu.roll(along * z, 1, 1)
    turned = pltpu.roll(across * z, FSIDE, 1)
    out = out - jnp.where(first, before, turned)
    if t + 1 < tiles:
        z_next = z_ref[:, tile(t + 1)]
        z_next_half = pltpu.roll(z_next, FSIDE, 1)
        out = out - across * jnp.where(first, z_half, z_next_half)
        return out, (z_next, z_next_half, turned)
    return out - across * z_half, None


def stencil_start(z_ref, fracs):
    z = z_ref[:, tile(0)]
    return z, pltpu.roll(z, FSIDE, 1), jnp.zeros((fracs, LANES), F32)


def sided(parity, even, odd):
    return jnp.where(parity == 0, odd, even), jnp.where(parity == 0, even, odd)


def near_sum(x, v_ref, ylo_ref, yhi_ref, wx_ref, wyp_ref, wym_ref, wzp_ref):
    v = v_ref[x + 1]
    depth = v.shape[0]
    row = iota(v.shape, 0)
    up = jnp.where(row == depth - 1, yhi_ref[pl.ds(x, 1), :], pltpu.roll(v, depth - 1, 0))
    down = jnp.where(row == 0, ylo_ref[pl.ds(x, 1), :], pltpu.roll(v, 1, 0))
    wz = wzp_ref[x]
    total = wx_ref[x + 1] * v_ref[x + 2] + wx_ref[x] * v_ref[x]
    total = total + wyp_ref[x] * up + wym_ref[x] * down
    return v, total + wz * pltpu.roll(v, LANES - 1, 1) + pltpu.roll(wz * v, 1, 1)


def planes(count, body, unroll=4):
    lax.fori_loop(0, count, lambda x, c: (body(x), c)[1], 0, unroll=unroll)


def restrict(values_ref, agg_ref, low_ref, high_ref, sums_ref):
    count, depth, _ = values_ref.shape
    sums_ref[...] = jnp.zeros(sums_ref.shape, F32)

    def plane(x):
        low = low_ref[x, 0]
        chunks = lax.div(high_ref[x, 0] - low + CHUNK, CHUNK)

        def body(c, carry):
            base = low + c * CHUNK
            parts = []
            for half in range(depth // 8):
                value = values_ref[x, half * 8 : (half + 1) * 8, :]
                label = agg_ref[x, half * 8 : (half + 1) * 8, :] - base
                parts.append([jnp.where(label == a, value, 0.0) for a in range(CHUNK)])
            for a in range(CHUNK):
                sums_ref[base + a] += sum(part[a] for part in parts)
            return carry

        lax.fori_loop(0, chunks, body, 0)

    planes(count, plane, unroll=1)
    sub = iota((8, LANES), 0)
    groups = []
    for start in range(0, NAGG, 8):
        group = jnp.zeros((8, LANES), F32)
        for a in range(8):
            group = jnp.where(sub == a, jnp.sum(sums_ref[start + a], axis=0, keepdims=True), group)
        groups.append(group)
    groups = groups + [jnp.zeros((8, LANES), F32)] * (LANES // 8 - len(groups))
    table = jnp.concatenate(groups, 0)
    ones = jnp.ones((8, LANES), BF16)
    return sum(mm(ones, part, NT) for part in thirds(table))


def host_cells(cell_ref, g):
    rows = [cell_ref[pl.ds(g * GROUP + i, 1), :] for i in range(GROUP)]
    return jnp.concatenate(rows, 1).astype(jnp.int32) - 1


def host_rows(ref, g):
    return jnp.concatenate([ref[pl.ds(g * GROUP + i, 1), :] for i in range(GROUP)], 1)


def groups_of(count_ref):
    return lax.div(count_ref[0] + GROUP - 1, GROUP)


def host_spread(cell_ref, value_refs, groups, out_ref):
    rows = out_ref.shape[0]
    out_ref[...] = jnp.zeros(out_ref.shape, F32)

    def body(g, carry):
        cells = host_cells(cell_ref, g)
        slots = cells.shape[1]
        at = lax.shift_right_arithmetic(cells, 7)
        hot = (cells & (LANES - 1)) == iota((LANES, slots), 0)
        highs, lows = [], []
        for ref in value_refs:
            value = host_rows(ref, g)
            high = value.astype(BF16).astype(F32)
            highs.append(jnp.where(hot, high, 0.0).astype(BF16))
            lows.append(jnp.where(hot, value - high, 0.0).astype(BF16))
        right = jnp.concatenate(highs + lows, 0)
        width = len(highs) * LANES
        left = jnp.where(at == iota((rows, slots), 0), 1.0, 0.0).astype(BF16)
        found = mm(left, right, NT)
        out_ref[...] += found[:, :width] + found[:, width:]
        return carry

    lax.fori_loop(0, groups, body, 0)


def host_fetch(table, cell_ref, groups, out_ref):
    rows = table.shape[0]
    high, low = halves(table.T)
    left = jnp.concatenate([high, low], 0)
    out_ref[...] = jnp.zeros(out_ref.shape, F32)

    def body(g, carry):
        cells = host_cells(cell_ref, g)
        slots = cells.shape[1]
        at = lax.shift_right_arithmetic(cells, 7)
        right = jnp.where(at == iota((rows, slots), 0), 1.0, 0.0).astype(BF16)
        found = mm(left, right, (((1,), (0,)), ((), ())))
        found = found[:LANES] + found[LANES:]
        hot = (cells & (LANES - 1)) == iota((LANES, slots), 0)
        value = jnp.sum(jnp.where(hot, found, 0.0), axis=0, keepdims=True)
        for i in range(GROUP):
            out_ref[pl.ds(g * GROUP + i, 1), :] = value[:, i * LANES : (i + 1) * LANES]
        return carry

    lax.fori_loop(0, groups, body, 0)


def reorder(perm, rows):
    return sum(mm(perm, part, (((1,), (0,)), ((), ()))) for part in thirds(rows))


def padded_rows(parts):
    rows = sum(p.shape[0] for p in parts)
    return jnp.concatenate(list(parts) + [jnp.zeros((LANES - rows, LANES), F32)], 0)


def write_layers(parity_x, parity_y, xlo, xhi, ylo, yhi, xe_ref, xo_ref, ye_ref, yo_ref):
    xe_ref[...] = jnp.where(parity_x == 0, xhi, xlo)
    xo_ref[...] = jnp.where(parity_x == 0, xlo, xhi)
    rows = ylo.shape[0]
    ye_ref[0:rows, :] = jnp.where(parity_y == 0, yhi, ylo)
    yo_ref[0:rows, :] = jnp.where(parity_y == 0, ylo, yhi)


def rock_faces(
    k_ref, p_ref, st_ref, agg_ref, xe_ref, xo_ref, par_ref,
    wx_ref, wy_ref, wz_ref, base_ref, cbase_ref, edge_ref, low_ref, high_ref,
    kp_ref, mp_ref, ends_ref,
):
    nx, ny, _ = k_ref.shape
    rate = -0.5 * mobility_rate
    k_lo, k_hi = sided(par_ref[0], xe_ref[0:ny, :], xo_ref[0:ny, :])
    p_lo, p_hi = sided(par_ref[0], xe_ref[ny:, :], xo_ref[ny:, :])
    kp_ref[0] = k_lo
    kp_ref[nx + 1] = k_hi
    mp_ref[0] = k_lo * jnp.exp(rate * p_lo)
    mp_ref[nx + 1] = k_hi * jnp.exp(rate * p_hi)

    def scale(x):
        k = k_ref[x]
        m = k * jnp.exp(rate * p_ref[x])
        kp_ref[x + 1] = k
        mp_ref[x + 1] = m
        for i, value in enumerate((k, m)):
            edge_ref[i, pl.ds(x, 1), :] = value[0:1, :]
            edge_ref[2 + i, pl.ds(x, 1), :] = value[ny - 1 : ny, :]

    planes(nx, scale)
    row = iota((ny, LANES), 0)
    lane = iota((ny, LANES), 1)

    def face_x(x):
        wx_ref[x] = 2.0 * mp_ref[x] * mp_ref[x + 1] / (kp_ref[x] + kp_ref[x + 1])

    planes(nx + 1, face_x, unroll=3)

    def assemble(x):
        k, m = kp_ref[x + 1], mp_ref[x + 1]
        wyp = 2.0 * m * pltpu.roll(m, ny - 1, 0) / (k + pltpu.roll(k, ny - 1, 0))
        wyp = jnp.where(row < ny - 1, wyp, 0.0)
        wym = pltpu.roll(wyp, 1, 0)
        wzp = 2.0 * m * pltpu.roll(m, LANES - 1, 1) / (k + pltpu.roll(k, LANES - 1, 1))
        wzp = jnp.where(lane < LANES - 1, wzp, 0.0)
        wzm = pltpu.roll(wzp, 1, 1)
        wy_ref[x] = wyp
        wz_ref[x] = wzp
        store = st_ref[x]
        wxm, wxp = wx_ref[x], wx_ref[x + 1]
        base_ref[x] = store + wxm + wxp + wyp + wym + wzp + wzm
        label = agg_ref[x]
        coarse = store + jnp.where((x > 0) & (agg_ref[jnp.maximum(x - 1, 0)] == label), 0.0, wxm)
        coarse = coarse + jnp.where((x < nx - 1) & (agg_ref[jnp.minimum(x + 1, nx - 1)] == label), 0.0, wxp)
        coarse = coarse + jnp.where(pltpu.roll(label, ny - 1, 0) == label, 0.0, wyp)
        coarse = coarse + jnp.where(pltpu.roll(label, 1, 0) == label, 0.0, wym)
        coarse = coarse + jnp.where(pltpu.roll(label, LANES - 1, 1) == label, 0.0, wzp)
        coarse = coarse + jnp.where(pltpu.roll(label, 1, 1) == label, 0.0, wzm)
        cbase_ref[x] = coarse
        ends_ref[0, pl.ds(x, 1), :] = jnp.min(label.astype(F32), axis=0, keepdims=True)
        ends_ref[1, pl.ds(x, 1), :] = jnp.max(label.astype(F32), axis=0, keepdims=True)

    planes(nx, assemble, unroll=2)
    low = jnp.min(ends_ref[0], axis=1, keepdims=True)
    high = jnp.max(ends_ref[1], axis=1, keepdims=True)
    low_ref[...] = jnp.broadcast_to(low, low_ref.shape).astype(jnp.int32)
    high_ref[...] = jnp.broadcast_to(high, high_ref.shape).astype(jnp.int32)


def rock_setup(
    b_ref, own_ref, wy_ref, base_ref, cbase_ref, edge_ref, ye_ref, yo_ref, par_ref,
    wyp_ref, wym_ref, dg_ref, z_ref, flow_ref, cc_ref, cell_ref, perm_ref, unperm_ref, count_ref,
    mxe_ref, mxo_ref, mye_ref, myo_ref,
    cv_ref, fv_ref, grid_ref, elo_ref, ehi_ref, ylo_ref, yhi_ref,
):
    nx, ny, _ = b_ref.shape
    fracs = own_ref.shape[0] // 3
    px, py = par_ref[0], par_ref[1]
    rate = -0.5 * mobility_rate

    even, odd = ye_ref[2 * nx :, :], yo_ref[2 * nx :, :]
    below, above = sided(py, even, odd)
    own = own_ref[...]

    def sources(i):
        part = slice(i * fracs, (i + 1) * fracs)
        return padded_rows([own[part], below[part], above[part]])

    cells = sources(0)
    active = jnp.broadcast_to((cells.T)[0:1, :], (8, LANES)) > 0.0
    hot = jnp.where(active, 1.0, 0.0)
    upto = jnp.where(iota((LANES, LANES), 0) <= iota((LANES, LANES), 1), 1.0, 0.0).astype(BF16)
    rank = mm(hot.astype(BF16), upto, (((1,), (0,)), ((), ())))
    place = jnp.where(active, rank, 0.0)[0:1, :].astype(jnp.int32)
    perm = jnp.where(place == iota((LANES, LANES), 0) + 1, 1.0, 0.0)
    perm_ref[...] = perm
    unperm_ref[...] = perm.T
    perm = perm.astype(BF16)
    count_ref[0] = jnp.sum(hot[0:1, :]).astype(jnp.int32)
    cell_ref[...] = reorder(perm, cells)
    cv_ref[...] = reorder(perm, sources(1))
    fv_ref[...] = reorder(perm, sources(2))
    host_spread(cell_ref, (cv_ref, fv_ref), groups_of(count_ref), grid_ref)

    k_lo, k_hi = sided(py, ye_ref[0:nx, :], yo_ref[0:nx, :])
    p_lo, p_hi = sided(py, ye_ref[nx : 2 * nx, :], yo_ref[nx : 2 * nx, :])
    elo_ref[...] = 2.0 * edge_ref[1] * (k_lo * jnp.exp(rate * p_lo)) / (edge_ref[0] + k_lo)
    ehi_ref[...] = 2.0 * edge_ref[3] * (k_hi * jnp.exp(rate * p_hi)) / (edge_ref[2] + k_hi)
    row = iota((ny, LANES), 0)

    def assemble(x):
        wyp = wy_ref[x]
        low = jnp.where(row == 0, elo_ref[pl.ds(x, 1), :], 0.0)
        high = jnp.where(row == ny - 1, ehi_ref[pl.ds(x, 1), :], 0.0)
        wyp_ref[x] = wyp + high
        wym_ref[x] = pltpu.roll(wyp, 1, 0) + low
        at = pl.ds(pl.multiple_of(x * ny, ny), ny)
        extra = grid_ref[at, 0:LANES] + low + high
        flow_ref[x] = grid_ref[at, LANES:]
        diag = base_ref[x] + extra
        dg_ref[x] = diag
        z = relaxation * b_ref[x] / diag
        z_ref[x] = z
        ylo_ref[pl.ds(x, 1), :] = z[0:1, :]
        yhi_ref[pl.ds(x, 1), :] = z[ny - 1 : ny, :]
        cc_ref[x] = cbase_ref[x] + extra

    planes(nx, assemble)
    write_layers(
        px, py, z_ref[0], z_ref[nx - 1], ylo_ref[...], yhi_ref[...], mxe_ref, mxo_ref, mye_ref, myo_ref
    )


def coarse_setup(cc_ref, agg_ref, low_ref, high_ref, cd_ref, sums_ref):
    sums = restrict(cc_ref, agg_ref, low_ref, high_ref, sums_ref)
    cd_ref[...] = jnp.where(iota((8, LANES), 1) < NAGG, sums, 1.0)


def fill_halo(vp_ref, v_ref, ylo_ref, yhi_ref, px, py, xe_ref, xo_ref, ye_ref, yo_ref):
    nx, ny, _ = v_ref.shape
    low, high = sided(px, xe_ref[...], xo_ref[...])
    vp_ref[0] = low
    vp_ref[nx + 1] = high

    def copy(x):
        vp_ref[x + 1] = v_ref[x]

    planes(nx, copy)
    low, high = sided(py, ye_ref[0:nx, :], yo_ref[0:nx, :])
    ylo_ref[...] = low
    yhi_ref[...] = high


def coarse_step(
    px, py, r_ref, z_ref, flow_of, agg_ref, weights, cd_ref, cell_ref, unperm_ref, scalars,
    p_ref, hv_ref, messages, vp_ref, ylo_ref, yhi_ref, s_ref, hc_ref, sums_ref,
):
    nx, ny, _ = z_ref.shape
    fracs = hv_ref.shape[0]
    count_ref, low_ref, high_ref = scalars

    def residual(x):
        v, near = near_sum(x, vp_ref, ylo_ref, yhi_ref, *weights)
        s_ref[x] = (1.0 - relaxation) * r_ref[x] + near + flow_of(x)

    planes(nx, residual)
    solved = restrict(s_ref, agg_ref, low_ref, high_ref, sums_ref) / cd_ref[...]

    def correct(x):
        z = vp_ref[x + 1]
        label = agg_ref[x]
        parts = [lane_pick(solved, label[h * 8 : (h + 1) * 8, :]) for h in range(ny // 8)]
        p = z + jnp.concatenate(parts, 0)
        p_ref[x] = p
        s_ref[x] = p
        ylo_ref[pl.ds(x, 1), :] = p[0:1, :]
        yhi_ref[pl.ds(x, 1), :] = p[ny - 1 : ny, :]

    planes(nx, correct)
    table = s_ref[...].reshape(nx * ny, LANES)
    host_fetch(table, cell_ref, groups_of(count_ref), hc_ref)
    values = reorder(unperm_ref[...].astype(BF16), hc_ref[...])
    hv_ref[...] = values[0:fracs]
    below, above = values[fracs : 2 * fracs], values[2 * fracs : 3 * fracs]
    write_layers(px, py, s_ref[0], s_ref[nx - 1], ylo_ref[...], yhi_ref[...], *messages)
    ye_ref, yo_ref = messages[2], messages[3]
    ye_ref[nx:, :] = jnp.where(py == 0, above, below)
    yo_ref[nx:, :] = jnp.where(py == 0, below, above)


def precond_first(
    b_ref, z_ref, flow_ref, agg_ref, wx_ref, wyp_ref, wym_ref, wzp_ref, cd_ref, cell_ref, unperm_ref,
    xe_ref, xo_ref, ye_ref, yo_ref, par_ref, count_ref, low_ref, high_ref,
    p_ref, hv_ref, mxe_ref, mxo_ref, mye_ref, myo_ref,
    vp_ref, ylo_ref, yhi_ref, s_ref, hc_ref, sums_ref,
):
    px, py = par_ref[0], par_ref[1]
    fill_halo(vp_ref, z_ref, ylo_ref, yhi_ref, px, py, xe_ref, xo_ref, ye_ref, yo_ref)
    coarse_step(
        px, py, b_ref, z_ref, lambda x: flow_ref[x], agg_ref, (wx_ref, wyp_ref, wym_ref, wzp_ref),
        cd_ref, cell_ref, unperm_ref, (count_ref, low_ref, high_ref), p_ref, hv_ref,
        (mxe_ref, mxo_ref, mye_ref, myo_ref), vp_ref, ylo_ref, yhi_ref, s_ref, hc_ref, sums_ref,
    )


def hosted_values(hv_ref, off_ref, py, ye_ref, yo_ref, nx):
    below, above = sided(py, ye_ref[nx:, :], yo_ref[nx:, :])
    offsets = off_ref[...]
    return jnp.where(offsets == 0, hv_ref[...], jnp.where(offsets == 1, above, below))


def image_first(
    p_ref, flow_ref, wx_ref, wyp_ref, wym_ref, wzp_ref, dg_ref, hv_ref, off_ref,
    fd_ref, q_ref, cpl_ref, cell_ref, xe_ref, xo_ref, ye_ref, yo_ref, par_ref,
    u_ref, z_ref, uf_ref, zn_ref, flux_ref, mxe_ref, mxo_ref, mye_ref, myo_ref,
    vp_ref, ylo_ref, yhi_ref, ylo_out_ref, yhi_out_ref, slot_ref, spread_ref,
):
    nx, ny, _ = p_ref.shape
    fracs, width = q_ref.shape
    tiles = width // LANES
    px, py = par_ref[0], par_ref[1]
    fill_halo(vp_ref, p_ref, ylo_ref, yhi_ref, px, py, xe_ref, xo_ref, ye_ref, yo_ref)
    weights = (wx_ref, wyp_ref, wym_ref, wzp_ref)

    def image(x):
        v, near = near_sum(x, vp_ref, ylo_ref, yhi_ref, *weights)
        diag = dg_ref[x]
        u = diag * v - near - flow_ref[x]
        u_ref[x] = u
        z = relaxation * u / diag
        z_ref[x] = z
        ylo_out_ref[pl.ds(x, 1), :] = z[0:1, :]
        yhi_out_ref[pl.ds(x, 1), :] = z[ny - 1 : ny, :]

    planes(nx, image)

    slot_ref[...] = cpl_ref[...] * hosted_values(hv_ref, off_ref, py, ye_ref, yo_ref, nx)
    slab_spread(cell_ref, slot_ref, spread_ref, tiles)
    for t in range(tiles):
        out = q_ref[:, tile(t)] - spread_ref[pl.ds(t, fracs, stride=tiles), :]
        uf_ref[:, tile(t)] = out
        zn_ref[:, tile(t)] = relaxation * out / fd_ref[:, tile(t)]
    flux = cpl_ref[...] * slab_pick(lambda t: zn_ref[:, tile(t)], cell_ref[...], tiles)
    flux_ref[...] = flux

    write_layers(
        px, py, z_ref[0], z_ref[nx - 1], ylo_out_ref[...], yhi_out_ref[...], mxe_ref, mxo_ref, mye_ref, myo_ref
    )
    mye_ref[nx:, :] = flux
    myo_ref[nx:, :] = flux


def precond_second(
    u_ref, z_ref, flux_ref, agg_ref, wx_ref, wyp_ref, wym_ref, wzp_ref, cd_ref, cell_ref, perm_ref, unperm_ref,
    xe_ref, xo_ref, ye_ref, yo_ref, par_ref, count_ref, low_ref, high_ref,
    p_ref, hv_ref, flow_ref, mxe_ref, mxo_ref, mye_ref, myo_ref,
    vp_ref, ylo_ref, yhi_ref, s_ref, hc_ref, fv_ref, grid_ref, sums_ref,
):
    nx, ny, _ = z_ref.shape
    px, py = par_ref[0], par_ref[1]
    fill_halo(vp_ref, z_ref, ylo_ref, yhi_ref, px, py, xe_ref, xo_ref, ye_ref, yo_ref)
    below, above = sided(py, ye_ref[nx:, :], yo_ref[nx:, :])
    fv_ref[...] = reorder(perm_ref[...].astype(BF16), padded_rows([flux_ref[...], below, above]))
    host_spread(cell_ref, (fv_ref,), groups_of(count_ref), grid_ref)

    def flow_of(x):
        flow = grid_ref[pl.ds(pl.multiple_of(x * ny, ny), ny), :]
        flow_ref[x] = flow
        return flow

    coarse_step(
        px, py, u_ref, z_ref, flow_of, agg_ref, (wx_ref, wyp_ref, wym_ref, wzp_ref),
        cd_ref, cell_ref, unperm_ref, (count_ref, low_ref, high_ref), p_ref, hv_ref,
        (mxe_ref, mxo_ref, mye_ref, myo_ref), vp_ref, ylo_ref, yhi_ref, s_ref, hc_ref, sums_ref,
    )


def frac_second(
    fd_ref, al_ref, ac_ref, z_ref, xc_ref, pairs_ref,
    q_ref,
    cross_ref, hot_ref,
):
    fracs, width = z_ref.shape
    tiles = width // LANES
    rows_at, lane_at = cross_place(pairs_ref, fracs)
    cross_hot(rows_at, hot_ref)
    ends = cross_pick(lambda t: z_ref[:, tile(t)], tiles, hot_ref, lane_at)
    cross_spread(xc_ref[...] * ends_swapped(ends), hot_ref, lane_at, cross_ref)
    first = iota((fracs, LANES), 1) < FSIDE
    carry = stencil_start(z_ref, fracs)
    for t in range(tiles):
        out, carry = frac_stencil(t, tiles, fd_ref, al_ref, ac_ref, z_ref, first, carry)
        q_ref[:, tile(t)] = out - cross_ref[t * fracs : (t + 1) * fracs, :]


def sums_of(rock, frac):
    return jnp.sum(rock, axis=0, keepdims=True) + jnp.sum(frac, axis=0, keepdims=True)


def dots_first(b_ref, u_ref, bf_ref, uf_ref, sums_ref):
    nx, ny, _ = b_ref.shape
    fracs, width = bf_ref.shape

    def products(b, u, sums):
        return tuple(s + t for s, t in zip(sums, (b * b, u * b, u * u)))

    def plane(x, sums):
        return products(b_ref[x], u_ref[x], sums)

    rock = lax.fori_loop(0, nx, plane, tuple(jnp.zeros((ny, LANES), F32) for _ in range(3)), unroll=4)
    frac = tuple(jnp.zeros((fracs, LANES), F32) for _ in range(3))
    for t in range(width // LANES):
        frac = products(bf_ref[:, tile(t)], uf_ref[:, tile(t)], frac)
    sub = iota((8, LANES), 0)
    table = jnp.zeros((8, LANES), F32)
    for i in range(3):
        table = jnp.where(sub == i, sums_of(rock[i], frac[i]), table)
    sums_ref[...] = table


def image_second(
    p_ref, flow_ref, wx_ref, wyp_ref, wym_ref, wzp_ref, dg_ref, b_ref, u_ref, hv_ref, off_ref,
    q_ref, cpl_ref, cell_ref, bf_ref, uf_ref, first_ref, xe_ref, xo_ref, ye_ref, yo_ref, par_ref,
    sums_ref,
    vp_ref, ylo_ref, yhi_ref, slot_ref, spread_ref,
):
    nx, ny, _ = p_ref.shape
    fracs, width = q_ref.shape
    tiles = width // LANES
    px, py = par_ref[0], par_ref[1]
    fill_halo(vp_ref, p_ref, ylo_ref, yhi_ref, px, py, xe_ref, xo_ref, ye_ref, yo_ref)
    weights = (wx_ref, wyp_ref, wym_ref, wzp_ref)

    def image(x, sums):
        v, near = near_sum(x, vp_ref, ylo_ref, yhi_ref, *weights)
        w = dg_ref[x] * v - near - flow_ref[x]
        return tuple(s + t for s, t in zip(sums, (w * b_ref[x], w * u_ref[x], w * w)))

    rock = lax.fori_loop(0, nx, image, tuple(jnp.zeros((ny, LANES), F32) for _ in range(3)), unroll=4)
    slot_ref[...] = cpl_ref[...] * hosted_values(hv_ref, off_ref, py, ye_ref, yo_ref, nx)
    slab_spread(cell_ref, slot_ref, spread_ref, tiles)
    frac = [jnp.zeros((fracs, LANES), F32) for _ in range(3)]
    for t in range(tiles):
        w = q_ref[:, tile(t)] - spread_ref[pl.ds(t, fracs, stride=tiles), :]
        frac = [s + t_ for s, t_ in zip(frac, (w * bf_ref[:, tile(t)], w * uf_ref[:, tile(t)], w * w))]
    sub = iota((8, LANES), 0)
    table = first_ref[...]
    for i in range(3):
        table = jnp.where(sub == i + 3, sums_of(rock[i], frac[i]), table)
    table = jnp.concatenate([table, jnp.zeros((LANES - 8, LANES), F32)], 0)
    ones = jnp.ones((8, LANES), BF16)
    row = sum(mm(ones, part, NT) for part in thirds(table))[0:1, :]
    sums_ref[...] = jnp.broadcast_to(row, sums_ref.shape)


def finish(all_ref, p_ref, q_ref, pf_ref, qf_ref, rock_ref, frac_ref, res_ref):
    total = jnp.sum(all_ref[...], axis=0, keepdims=True)
    total = jnp.broadcast_to(total, (8, LANES))
    bb, ub, uu, wb, wu, ww = (
        lane_pick(total, jnp.full((8, LANES), i, jnp.int32)) for i in range(6)
    )
    norm2 = bb + epsilon
    norm = jnp.sqrt(norm2)
    h00 = ub / norm2
    n1 = jnp.maximum(uu - 2.0 * h00 * ub + h00 * h00 * bb, 0.0) / norm2
    h10 = jnp.sqrt(n1 + epsilon)
    h01 = (wb - h00 * ub) / (norm2 * h10)
    h11 = (wu - h00 * wb - h00 * uu + h00 * h00 * ub) / (norm2 * h10 * h10)
    square = (ww - 2.0 * h00 * wu + h00 * h00 * uu) / (norm2 * h10 * h10)
    v00 = bb / norm2
    v11 = n1 / (h10 * h10)
    v01 = (ub - h00 * bb) / (norm2 * h10)
    n2 = square + h01 * h01 * (v00 - 2.0) + h11 * h11 * (v11 - 2.0) + 2.0 * h01 * h11 * v01
    h21 = jnp.sqrt(jnp.maximum(n2, epsilon * square) + epsilon)
    r0 = jnp.sqrt(h00 * h00 + h10 * h10)
    c0, s0 = h00 / r0, h10 / r0
    top = c0 * h01 + s0 * h11
    low = c0 * h11 - s0 * h01
    r1 = jnp.sqrt(low * low + h21 * h21)
    c1, s1 = low / r1, h21 / r1
    g0, g1 = c0 * norm, -s0 * norm
    y1 = c1 * g1 / r1
    y0 = (g0 - top * y1) / r0
    residual = jnp.abs(s1 * g1)
    beta = y1 / (norm * h10)
    alpha = y0 / norm - h00 * beta
    res_ref[0, 0] = residual[0, 0]
    nx, ny, _ = p_ref.shape
    alpha_y, beta_y = alpha[0:1, :], beta[0:1, :]

    def rock(x):
        rock_ref[x] = alpha_y * p_ref[x] + beta_y * q_ref[x]

    planes(nx, rock)
    for t in range(pf_ref.shape[1] // LANES):
        frac_ref[:, tile(t)] = alpha_y * pf_ref[:, tile(t)] + beta_y * qf_ref[:, tile(t)]


def local(
    rock_rhs,
    frac_rhs,
    perm,
    storage,
    pressure,
    frac_perm,
    frac_storage,
    frac_pressure,
    couple_geom,
    couple_count,
    couple_frac_cell,
    couple_rock_cell,
    host_offset,
    cross_pairs,
    cross_geom,
    aggregates,
):
    nx, ny, nz = rock_rhs.shape
    fracs, width = frac_rhs.shape
    pairs = cross_pairs.shape[1]
    tiles = width // LANES
    cube, slab, slots = shaped(nx, ny, nz), shaped(fracs, width), shaped(fracs, LANES)
    gx, gy = lax.axis_index("gx"), lax.axis_index("gy")
    parity = jnp.stack([gx % 2, gy % 2]).astype(jnp.int32)
    vcube = pltpu.VMEM((nx, ny, nz), F32)
    vpad = pltpu.VMEM((nx + 2, ny, nz), F32)
    vside = pltpu.VMEM((nx, nz), F32)
    vhost = pltpu.VMEM((LANES, LANES), F32)
    vcross = pltpu.VMEM((fracs * tiles, LANES), F32)
    vhot = pltpu.VMEM((fracs * tiles, 2 * pairs), BF16)
    vslots = pltpu.VMEM((fracs, LANES), F32)

    even_x = gx % 2 == 0
    x_lo = jnp.concatenate([a[0] for a in (perm, pressure)], 0)
    x_hi = jnp.concatenate([a[nx - 1] for a in (perm, pressure)], 0)
    x_even, x_odd = exchange(jnp.where(even_x, x_hi, x_lo), jnp.where(even_x, x_lo, x_hi), "gx")

    message = shaped(2 * nx + 3 * fracs, LANES)
    al, ac, fd, zf, cpl, xc, own, y_even, y_odd, off = call(
        frac_setup,
        [slab, slab, slab, slab, slots, shaped(1, 2 * pairs), shaped(3 * fracs, LANES), message, message]
        + [shaped(fracs, LANES, dtype=jnp.int32)],
        [
            frac_rhs, frac_perm, frac_storage, frac_pressure, couple_geom, couple_frac_cell, couple_rock_cell,
            cross_pairs, cross_geom.reshape(1, pairs), couple_count, host_offset, perm, pressure, parity,
        ],
        [vcross, vcross, vhot, pltpu.VMEM((4, nx, nz), F32), pltpu.SemaphoreType.DMA((4,))],
        smem_in=(9, 10, 13),
        hbm_in=(11, 12),
        limit=62,
    )
    y_even, y_odd = exchange(y_even, y_odd, "gy")

    layers = [shaped(ny, nz), shaped(ny, nz)]
    count_shape = shaped(1, dtype=jnp.int32)
    host_shape = shaped(LANES, LANES)
    range_shape = shaped(nx, LANES, dtype=jnp.int32)
    wx, wy, wzp, base, cbase, edge, low, high = call(
        rock_faces,
        [shaped(nx + 1, ny, nz), cube, cube, cube, cube, shaped(4, nx, nz), range_shape, range_shape],
        [perm, pressure, storage, aggregates, x_even, x_odd, parity],
        [vpad, vpad, pltpu.VMEM((2, nx, nz), F32)],
        smem_in=(6,),
    )
    wyp, wym, dg, z0, flow0, cc, cells, pack, unpack, count, xe, xo, ye, yo = call(
        rock_setup,
        [cube] * 6 + [host_shape] * 3 + [count_shape] + layers + [shaped(nx, nz)] * 2,
        [rock_rhs, own, wy, base, cbase, edge, y_even, y_odd, parity],
        [vhost, vhost, pltpu.VMEM((nx * ny, 2 * LANES), F32), vside, vside, vside, vside],
        smem_in=(8,),
        smem_out=(9,),
    )
    vsums = pltpu.VMEM((NAGG + CHUNK, 8, LANES), F32)
    weights = [wx, wyp, wym, wzp]
    xe, xo = exchange(xe, xo, "gx")
    ye, yo = exchange(ye, yo, "gy")
    (cd,) = call(
        coarse_setup, [shaped(8, LANES)], [cc, aggregates, low, high], [vsums], smem_in=(2, 3)
    )
    p0, hv, xe, xo, ye, yo = call(
        precond_first,
        [cube, slots] + layers + [shaped(nx + fracs, nz)] * 2,
        [rock_rhs, z0, flow0, aggregates] + weights + [cd, cells, unpack, xe, xo, ye, yo, parity, count, low, high],
        [vpad, vside, vside, vcube, vhost, vsums],
        smem_in=(15, 16, 17, 18),
    )
    xe, xo = exchange(xe, xo, "gx")
    ye, yo = exchange(ye, yo, "gy")
    (q0,) = call(frac_second, [slab], [fd, al, ac, zf, xc, cross_pairs], [vcross, vhot])
    u0, z1, uf0, zf1, flux1, xe, xo, ye, yo = call(
        image_first,
        [cube, cube, slab, slab, slots] + layers + [shaped(nx + fracs, nz)] * 2,
        [p0, flow0] + weights + [dg, hv, off, fd, q0, cpl, couple_frac_cell, xe, xo, ye, yo, parity],
        [vpad, vside, vside, vside, vside, vslots, vcross],
        smem_in=(17,),
    )
    xe, xo = exchange(xe, xo, "gx")
    ye, yo = exchange(ye, yo, "gy")
    (q1,) = call(frac_second, [slab], [fd, al, ac, zf1, xc, cross_pairs], [vcross, vhot])
    p1, hv, flow1, xe, xo, ye, yo = call(
        precond_second,
        [cube, slots, cube] + layers + [shaped(nx + fracs, nz)] * 2,
        [u0, z1, flux1, aggregates] + weights + [cd, cells, pack, unpack, xe, xo, ye, yo, parity, count, low, high],
        [vpad, vside, vside, vcube, vhost, vhost, pltpu.VMEM((nx * ny, LANES), F32), vsums],
        smem_in=(16, 17, 18, 19),
    )
    xe, xo = exchange(xe, xo, "gx")
    ye, yo = exchange(ye, yo, "gy")
    (first,) = call(dots_first, [shaped(8, LANES)], [rock_rhs, u0, frac_rhs, uf0])
    devices = lax.axis_size("gx") * lax.axis_size("gy")
    (sums,) = call(
        image_second,
        [shaped(devices, LANES)],
        [p1, flow1] + weights + [dg, rock_rhs, u0, hv, off, q1, cpl, couple_frac_cell, frac_rhs, uf0, first, xe, xo, ye, yo, parity],
        [vpad, vside, vside, vslots, vcross],
        smem_in=(21,),
    )
    gathered = lax.all_to_all(sums, ("gx", "gy"), 0, 0, tiled=True)
    rock_update, frac_update, residual = call(
        finish,
        [cube, slab, shaped(1, 1)],
        [gathered, p0, p1, zf, zf1],
        smem_out=(2,),
    )
    return rock_update, frac_update, residual.reshape(())


def solution(mesh):
    placed = (
        P("gx", "gy", None),
        P(("gx", "gy"), None),
        P("gx", "gy", None),
        P("gx", "gy", None),
        P("gx", "gy", None),
        P(("gx", "gy"), None),
        P(("gx", "gy"), None),
        P(("gx", "gy"), None),
        P(("gx", "gy"), None),
        P(("gx", "gy")),
        P(("gx", "gy"), None),
        P(("gx", "gy"), None),
        P(("gx", "gy")),
        P(None, ("gx", "gy")),
        P(("gx", "gy")),
        P("gx", "gy", None),
    )
    return jax.shard_map(
        local,
        mesh=mesh,
        in_specs=placed,
        out_specs=(P("gx", "gy", None), P(("gx", "gy"), None), P()),
        check_vma=False,
    )
```

```python
import functools

import jax
import jax.numpy as jnp
from jax import lax
from jax.experimental import pallas as pl
from jax.experimental.pallas import tpu as pltpu
from jax.sharding import PartitionSpec as P

FSIDE = 64
NAGG = 64
LANES = 128
GROUP = 4
CHUNK = 8
PACK = 40

mobility_rate = 0.5
relaxation = 0.8
epsilon = 1e-06
F32 = jnp.float32
BF16 = jnp.bfloat16
NT = (((1,), (1,)), ((), ()))
TN = (((0,), (0,)), ((), ()))
VM = pl.BlockSpec(memory_space=pltpu.VMEM)
SM = pl.BlockSpec(memory_space=pltpu.SMEM)
HB = pl.BlockSpec(memory_space=pltpu.HBM)


def call(kernel, outs, ins, scratch=(), flops=1 << 24, smem_in=(), smem_out=(), hbm_in=(), hbm_out=(), limit=24):
    nbytes = sum(a.size * a.dtype.itemsize for a in list(ins) + list(outs))
    return pl.pallas_call(
        kernel,
        out_shape=tuple(outs),
        in_specs=[SM if i in smem_in else HB if i in hbm_in else VM for i in range(len(ins))],
        out_specs=tuple(SM if i in smem_out else HB if i in hbm_out else VM for i in range(len(outs))),
        scratch_shapes=list(scratch),
        cost_estimate=pl.CostEstimate(flops=flops, bytes_accessed=nbytes, transcendentals=0),
        compiler_params=pltpu.CompilerParams(vmem_limit_bytes=limit << 20),
    )(*ins)


def shaped(*dims, dtype=F32):
    return jax.ShapeDtypeStruct(dims, dtype)


def swap_pairs(n):
    even = [(i, i ^ 1) for i in range(n) if i ^ 1 < n]
    odd = [(i, ((i - 1) ^ 1) + 1) for i in range(1, n) if ((i - 1) ^ 1) + 1 < n]
    return even, odd


def exchange(even_msg, odd_msg, axis):
    even, odd = swap_pairs(lax.axis_size(axis))
    return lax.ppermute(even_msg, axis, even), lax.ppermute(odd_msg, axis, odd)


def halves(value):
    high = value.astype(BF16)
    return high, (value - high.astype(F32)).astype(BF16)


def thirds(value):
    high = value.astype(BF16)
    rest = value - high.astype(F32)
    mid = rest.astype(BF16)
    return high, mid, (rest - mid.astype(F32)).astype(BF16)


def mm(lhs, rhs, dims):
    return lax.dot_general(lhs, rhs, dims, preferred_element_type=F32)


def iota(shape, dim):
    return lax.broadcasted_iota(jnp.int32, shape, dim)


def lane_pick(table, index):
    return jnp.take_along_axis(table, index, axis=1)


def tile(t):
    return slice(t * LANES, (t + 1) * LANES)


def slab_pick(load, cells, tiles):
    at_lane = cells & (LANES - 1)
    at_tile = lax.shift_right_logical(cells, 7)
    result = jnp.zeros(cells.shape, F32)
    for t in range(tiles):
        result = jnp.where(at_tile == t, lane_pick(load(t), at_lane), result)
    return result


def slab_spread(cell_ref, value_ref, out_ref, tiles):
    fracs = cell_ref.shape[0]

    def body(f, carry):
        cells = cell_ref[pl.ds(f, 1), :]
        value = value_ref[pl.ds(f, 1), :]
        at = lax.shift_right_logical(cells, 7) == iota((tiles, LANES), 0)
        left = jnp.concatenate(halves(jnp.where(at, value, 0.0)), 0)
        hot = jnp.where((cells & (LANES - 1)) == iota((LANES, LANES), 0), 1.0, 0.0).astype(BF16)
        found = mm(left, hot, NT)
        out_ref[pl.ds(pl.multiple_of(f * tiles, tiles), tiles), :] = found[:tiles] + found[tiles:]
        return carry

    lax.fori_loop(0, fracs, body, 0, unroll=True)


def cross_hot(rows_at, hot_ref):
    rows, ends = hot_ref.shape
    step = 128

    def body(j, carry):
        base = pl.multiple_of(j * step, step)
        hot_ref[pl.ds(base, step), :] = jnp.where(rows_at == iota((step, ends), 0) + base, 1.0, 0.0).astype(BF16)
        return carry

    lax.fori_loop(0, rows // step, body, 0)


def cross_pick(load, tiles, hot_ref, lane_at):
    table = jnp.concatenate([load(t) for t in range(tiles)], 0)
    high, low = halves(table)
    both = jnp.concatenate([high, low], 1)
    found = mm(both, hot_ref[...], TN)
    found = found[:LANES] + found[LANES:]
    hot = lane_at == iota(found.shape, 0)
    return jnp.sum(jnp.where(hot, found, 0.0), axis=0, keepdims=True)


def cross_spread(values, hot_ref, lane_at, out_ref):
    ends = hot_ref.shape[1]
    hot = lane_at == iota((LANES, ends), 0)
    right = jnp.concatenate(halves(jnp.where(hot, values, 0.0)), 0)
    found = mm(hot_ref[...], right, NT)
    out_ref[...] = found[:, :LANES] + found[:, LANES:]


def ends_swapped(values):
    half = values.shape[1] // 2
    return jnp.concatenate([values[:, half:], values[:, :half]], 1)


def cross_place(pairs_ref, fracs):
    pairs = jnp.concatenate([pairs_ref[0:1, :], pairs_ref[1:2, :]], 1)
    owner = lax.shift_right_logical(pairs, 12)
    row = (lax.shift_right_logical(pairs, 7) & (FSIDE * FSIDE // LANES - 1)) * fracs + owner
    return row, pairs & (LANES - 1)


def place_slots(count_ref, offset_ref, place_ref, fracs):
    def body(f, ends):
        offset = offset_ref[f]
        here, up, down = ends
        count = count_ref[f]
        at = jnp.where(offset == 0, here, jnp.where(offset == 1, up, down))
        which = jnp.where(offset == 0, 0, jnp.where(offset == 1, 1, 2))
        place_ref[f] = at + which * (PACK * LANES)
        return (
            here + jnp.where(offset == 0, count, 0),
            up + jnp.where(offset == 1, count, 0),
            down + jnp.where(offset == -1, count, 0),
        )

    zero = jnp.int32(0)
    lax.fori_loop(0, fracs, body, (zero, zero, zero))


def pack_slots(place_ref, value_refs, packed_refs, fracs, unroll=True):
    lane = iota((1, LANES), 1)
    for packed in packed_refs:
        packed[...] = jnp.zeros(packed.shape, F32)

    def body(f, carry):
        place = place_ref[f]
        at, shift = lax.shift_right_logical(place, 7), place & (LANES - 1)
        for value, packed in zip(value_refs, packed_refs):
            turned = pltpu.roll(value[pl.ds(f, 1), :], shift, 1)
            packed[pl.ds(at, 1), :] = jnp.where(lane >= shift, turned, packed[pl.ds(at, 1), :])
            packed[pl.ds(at + 1, 1), :] = jnp.where(lane < shift, turned, 0.0)
        return carry

    lax.fori_loop(0, fracs, body, 0, unroll=unroll)


def unpack_slots(place_ref, packed_ref, value_ref, fracs):
    lane = iota((1, LANES), 1)

    def body(f, carry):
        place = place_ref[f]
        at, shift = lax.shift_right_logical(place, 7), place & (LANES - 1)
        both = jnp.where(lane >= shift, packed_ref[pl.ds(at, 1), :], packed_ref[pl.ds(at + 1, 1), :])
        value_ref[pl.ds(f, 1), :] = pltpu.roll(both, (LANES - shift) & (LANES - 1), 1)
        return carry

    lax.fori_loop(0, fracs, body, 0, unroll=True)


def frac_setup(
    b_hbm, k_hbm, st_hbm, p_hbm, geom_ref, cell_ref, rock_ref, pairs_ref, xgeom_ref, count_ref, offset_ref,
    perm_hbm, press_hbm, par_ref,
    al_hbm, ac_hbm, fd_hbm, z_hbm, cpl_ref, xc_ref, own_ref, even_ref, odd_ref, place_ref,
    spread_ref, cross_ref, hot_ref, b_ref, k_ref, st_ref, p_ref, al_ref, ac_ref, fd_ref, z_ref, m_ref,
    side_ref, where_ref, flux_ref, pack_where_ref, pack_cpl_ref, pack_flux_ref, sems,
):
    last = perm_hbm.shape[1] - 1
    copies = [
        pltpu.make_async_copy(source, target, sems.at[i])
        for i, (source, target) in enumerate(
            [
                (p_hbm, p_ref),
                (k_hbm, k_ref),
                (st_hbm, st_ref),
                (b_hbm, b_ref),
                (perm_hbm.at[:, 0, :], side_ref.at[0]),
                (press_hbm.at[:, 0, :], side_ref.at[1]),
                (perm_hbm.at[:, last, :], side_ref.at[2]),
                (press_hbm.at[:, last, :], side_ref.at[3]),
                (al_ref, al_hbm),
                (ac_ref, ac_hbm),
                (fd_ref, fd_hbm),
                (z_ref, z_hbm),
            ]
        )
    ]
    for copy in copies[:8]:
        copy.start()
    fracs, width = b_ref.shape
    tiles = width // LANES
    lane = iota((fracs, LANES), 1)
    row = iota((fracs, LANES), 0)
    inner = (lane & (FSIDE - 1)) < FSIDE - 1
    first = lane < FSIDE

    place_slots(count_ref, offset_ref, place_ref, fracs)
    counts = jnp.zeros((fracs, LANES), jnp.int32)
    for f in range(fracs):
        counts = jnp.where(row == f, count_ref[f], counts)
    live = lane < counts
    where_ref[...] = jnp.where(live, rock_ref[...].astype(F32) + 1.0, 0.0)
    cells = cell_ref[...]
    copies[0].wait()
    found = slab_pick(lambda t: p_ref[:, tile(t)], cells, tiles)
    coupling = jnp.where(live, geom_ref[...] * jnp.exp(-mobility_rate * found), 0.0)
    cpl_ref[...] = coupling
    slab_spread(cell_ref, cpl_ref, spread_ref, tiles)

    rows_at, lane_at = cross_place(pairs_ref, fracs)
    cross_hot(rows_at, hot_ref)
    ends = cross_pick(lambda t: p_ref[:, tile(t)], tiles, hot_ref, lane_at)
    geom = jnp.concatenate([xgeom_ref[...], xgeom_ref[...]], 1)
    xc = geom * jnp.exp(-0.5 * mobility_rate * (ends + ends_swapped(ends)))
    xc_ref[...] = xc
    cross_spread(xc, hot_ref, lane_at, cross_ref)

    for copy in copies[1:8]:
        copy.wait()

    for t in range(tiles):
        m_ref[:, tile(t)] = k_ref[:, tile(t)] * jnp.exp(-0.5 * mobility_rate * p_ref[:, tile(t)])
    for t in range(tiles):
        k, m = k_ref[:, tile(t)], m_ref[:, tile(t)]
        k_one, m_one = pltpu.roll(k, LANES - 1, 1), pltpu.roll(m, LANES - 1, 1)
        along = jnp.where(inner, 2.0 * m * m_one / (k + k_one), 0.0)
        al_ref[:, tile(t)] = along
        st_ref[:, tile(t)] = st_ref[:, tile(t)] + along + pltpu.roll(along, 1, 1)
    for t in range(tiles):
        k, m = k_ref[:, tile(t)], m_ref[:, tile(t)]
        if t + 1 < tiles:
            k_far = pltpu.roll(jnp.where(first, k_ref[:, tile(t + 1)], k), FSIDE, 1)
            m_far = pltpu.roll(jnp.where(first, m_ref[:, tile(t + 1)], m), FSIDE, 1)
            across = 2.0 * m * m_far / (k + k_far)
        else:
            k_far, m_far = pltpu.roll(k, FSIDE, 1), pltpu.roll(m, FSIDE, 1)
            across = jnp.where(first, 2.0 * m * m_far / (k + k_far), 0.0)
        ac_ref[:, tile(t)] = across
    for t in range(tiles):
        across = ac_ref[:, tile(t)]
        if t > 0:
            back = pltpu.roll(jnp.where(first, across, ac_ref[:, tile(t - 1)]), FSIDE, 1)
        else:
            back = jnp.where(first, 0.0, pltpu.roll(across, FSIDE, 1))
        diag = st_ref[:, tile(t)] + across + back
        diag = diag + spread_ref[pl.ds(t, fracs, stride=tiles), :] + cross_ref[t * fracs : (t + 1) * fracs, :]
        fd_ref[:, tile(t)] = diag
        z_ref[:, tile(t)] = relaxation * b_ref[:, tile(t)] / diag
    for copy in copies[8:]:
        copy.start()
    flux_ref[...] = coupling * slab_pick(lambda t: z_ref[:, tile(t)], cells, tiles)
    packs = (pack_where_ref, pack_cpl_ref, pack_flux_ref)
    pack_slots(place_ref, (where_ref, cpl_ref, flux_ref), packs, fracs, 4)
    sides = side_ref.shape[1]
    even_up = par_ref[1] == 0
    for ref, up in ((even_ref, even_up), (odd_ref, jnp.logical_not(even_up))):
        ref[0:sides, :] = jnp.where(up, side_ref[2], side_ref[0])
        ref[sides : 2 * sides, :] = jnp.where(up, side_ref[3], side_ref[1])
    for i, pack in enumerate(packs):
        part = slice(i * fracs, (i + 1) * fracs)
        own_ref[part, :] = pack[0:fracs, :]
        send = slice(2 * sides + i * fracs, 2 * sides + (i + 1) * fracs)
        even_ref[send, :], odd_ref[send, :] = directed(even_up, pack, fracs)
    for copy in copies[8:]:
        copy.wait()


def directed(even_up, pack, fracs):
    up, down = pack[PACK : PACK + fracs, :], pack[2 * PACK : 2 * PACK + fracs, :]
    return jnp.where(even_up, up, down), jnp.where(even_up, down, up)


def frac_stencil(t, tiles, fd_ref, al_ref, ac_ref, z_ref, first, carry):
    z, z_half, before = carry
    along, across = al_ref[:, tile(t)], ac_ref[:, tile(t)]
    out = fd_ref[:, tile(t)] * z - along * pltpu.roll(z, LANES - 1, 1) - pltpu.roll(along * z, 1, 1)
    turned = pltpu.roll(across * z, FSIDE, 1)
    out = out - jnp.where(first, before, turned)
    if t + 1 < tiles:
        z_next = z_ref[:, tile(t + 1)]
        z_next_half = pltpu.roll(z_next, FSIDE, 1)
        out = out - across * jnp.where(first, z_half, z_next_half)
        return out, (z_next, z_next_half, turned)
    return out - across * z_half, None


def stencil_start(z_ref, fracs):
    z = z_ref[:, tile(0)]
    return z, pltpu.roll(z, FSIDE, 1), jnp.zeros((fracs, LANES), F32)


def sided(parity, even, odd):
    return jnp.where(parity == 0, odd, even), jnp.where(parity == 0, even, odd)


def near_sum(x, v_ref, ylo_ref, yhi_ref, wx_ref, wyp_ref, wym_ref, wzp_ref):
    v = v_ref[x + 1]
    depth = v.shape[0]
    row = iota(v.shape, 0)
    up = jnp.where(row == depth - 1, yhi_ref[pl.ds(x, 1), :], pltpu.roll(v, depth - 1, 0))
    down = jnp.where(row == 0, ylo_ref[pl.ds(x, 1), :], pltpu.roll(v, 1, 0))
    wz = wzp_ref[x]
    total = wx_ref[x + 1] * v_ref[x + 2] + wx_ref[x] * v_ref[x]
    total = total + wyp_ref[x] * up + wym_ref[x] * down
    return v, total + wz * pltpu.roll(v, LANES - 1, 1) + pltpu.roll(wz * v, 1, 1)


def planes(count, body, unroll=4):
    lax.fori_loop(0, count, lambda x, c: (body(x), c)[1], 0, unroll=unroll)


def restrict(values_ref, agg_ref, low_ref, high_ref, sums_ref):
    count, depth, _ = values_ref.shape
    sums_ref[...] = jnp.zeros(sums_ref.shape, F32)

    def plane(x):
        low = low_ref[x, 0]
        chunks = lax.div(high_ref[x, 0] - low + CHUNK, CHUNK)

        def body(c, carry):
            base = low + c * CHUNK
            parts = []
            for half in range(depth // 8):
                value = values_ref[x, half * 8 : (half + 1) * 8, :]
                label = agg_ref[x, half * 8 : (half + 1) * 8, :] - base
                parts.append([jnp.where(label == a, value, 0.0) for a in range(CHUNK)])
            for a in range(CHUNK):
                sums_ref[base + a] += sum(part[a] for part in parts)
            return carry

        lax.fori_loop(0, chunks, body, 0)

    planes(count, plane, unroll=1)
    sub = iota((8, LANES), 0)
    groups = []
    for start in range(0, NAGG, 8):
        group = jnp.zeros((8, LANES), F32)
        for a in range(8):
            group = jnp.where(sub == a, jnp.sum(sums_ref[start + a], axis=0, keepdims=True), group)
        groups.append(group)
    groups = groups + [jnp.zeros((8, LANES), F32)] * (LANES // 8 - len(groups))
    table = jnp.concatenate(groups, 0)
    ones = jnp.ones((8, LANES), BF16)
    return sum(mm(ones, part, NT) for part in thirds(table))


def host_cells(cell_ref, g):
    rows = [cell_ref[pl.ds(g * GROUP + i, 1), :] for i in range(GROUP)]
    return jnp.concatenate(rows, 1).astype(jnp.int32) - 1


def host_rows(ref, g):
    return jnp.concatenate([ref[pl.ds(g * GROUP + i, 1), :] for i in range(GROUP)], 1)


def groups_of(count_ref):
    return lax.div(count_ref[0] + GROUP - 1, GROUP)


def host_spread(cell_ref, value_refs, groups, out_ref):
    rows = out_ref.shape[0]
    out_ref[...] = jnp.zeros(out_ref.shape, F32)

    def body(g, carry):
        cells = host_cells(cell_ref, g)
        slots = cells.shape[1]
        at = lax.shift_right_arithmetic(cells, 7)
        hot = (cells & (LANES - 1)) == iota((LANES, slots), 0)
        highs, lows = [], []
        for ref in value_refs:
            high, low = halves(jnp.where(hot, host_rows(ref, g), 0.0))
            highs.append(high)
            lows.append(low)
        right = jnp.concatenate(highs + lows, 0)
        width = len(highs) * LANES
        left = jnp.where(at == iota((rows, slots), 0), 1.0, 0.0).astype(BF16)
        found = mm(left, right, NT)
        out_ref[...] += found[:, :width] + found[:, width:]
        return carry

    lax.fori_loop(0, groups, body, 0)


def host_fetch(table, cell_ref, groups, out_ref):
    rows = table.shape[0]
    high, low = halves(table.T)
    left = jnp.concatenate([high, low], 0)
    out_ref[...] = jnp.zeros(out_ref.shape, F32)

    def body(g, carry):
        cells = host_cells(cell_ref, g)
        slots = cells.shape[1]
        at = lax.shift_right_arithmetic(cells, 7)
        right = jnp.where(at == iota((rows, slots), 0), 1.0, 0.0).astype(BF16)
        found = mm(left, right, (((1,), (0,)), ((), ())))
        found = found[:LANES] + found[LANES:]
        hot = (cells & (LANES - 1)) == iota((LANES, slots), 0)
        value = jnp.sum(jnp.where(hot, found, 0.0), axis=0, keepdims=True)
        for i in range(GROUP):
            out_ref[pl.ds(g * GROUP + i, 1), :] = value[:, i * LANES : (i + 1) * LANES]
        return carry

    lax.fori_loop(0, groups, body, 0)


def reorder(perm, rows):
    return sum(mm(perm, part, (((1,), (0,)), ((), ()))) for part in thirds(rows))


def padded_rows(parts):
    rows = sum(p.shape[0] for p in parts)
    return jnp.concatenate(list(parts) + [jnp.zeros((LANES - rows, LANES), F32)], 0)


def write_layers(parity_x, parity_y, xlo, xhi, ylo, yhi, xe_ref, xo_ref, ye_ref, yo_ref):
    xe_ref[...] = jnp.where(parity_x == 0, xhi, xlo)
    xo_ref[...] = jnp.where(parity_x == 0, xlo, xhi)
    rows = ylo.shape[0]
    ye_ref[0:rows, :] = jnp.where(parity_y == 0, yhi, ylo)
    yo_ref[0:rows, :] = jnp.where(parity_y == 0, ylo, yhi)


def rock_faces(
    k_ref, p_ref, st_ref, agg_ref, xe_ref, xo_ref, par_ref,
    wx_ref, wy_ref, wz_ref, base_ref, cbase_ref, edge_ref, low_ref, high_ref,
    kp_ref, mp_ref, ends_ref,
):
    nx, ny, _ = k_ref.shape
    rate = -0.5 * mobility_rate
    k_lo, k_hi = sided(par_ref[0], xe_ref[0:ny, :], xo_ref[0:ny, :])
    p_lo, p_hi = sided(par_ref[0], xe_ref[ny:, :], xo_ref[ny:, :])
    kp_ref[0] = k_lo
    kp_ref[nx + 1] = k_hi
    mp_ref[0] = k_lo * jnp.exp(rate * p_lo)
    mp_ref[nx + 1] = k_hi * jnp.exp(rate * p_hi)

    def scale(x):
        k = k_ref[x]
        m = k * jnp.exp(rate * p_ref[x])
        kp_ref[x + 1] = k
        mp_ref[x + 1] = m
        for i, value in enumerate((k, m)):
            edge_ref[i, pl.ds(x, 1), :] = value[0:1, :]
            edge_ref[2 + i, pl.ds(x, 1), :] = value[ny - 1 : ny, :]

    planes(nx, scale)
    row = iota((ny, LANES), 0)
    lane = iota((ny, LANES), 1)

    def face_x(x):
        wx_ref[x] = 2.0 * mp_ref[x] * mp_ref[x + 1] / (kp_ref[x] + kp_ref[x + 1])

    planes(nx + 1, face_x, unroll=3)

    def assemble(x):
        k, m = kp_ref[x + 1], mp_ref[x + 1]
        wyp = 2.0 * m * pltpu.roll(m, ny - 1, 0) / (k + pltpu.roll(k, ny - 1, 0))
        wyp = jnp.where(row < ny - 1, wyp, 0.0)
        wym = pltpu.roll(wyp, 1, 0)
        wzp = 2.0 * m * pltpu.roll(m, LANES - 1, 1) / (k + pltpu.roll(k, LANES - 1, 1))
        wzp = jnp.where(lane < LANES - 1, wzp, 0.0)
        wzm = pltpu.roll(wzp, 1, 1)
        wy_ref[x] = wyp
        wz_ref[x] = wzp
        store = st_ref[x]
        wxm, wxp = wx_ref[x], wx_ref[x + 1]
        base_ref[x] = store + wxm + wxp + wyp + wym + wzp + wzm
        label = agg_ref[x]
        coarse = store + jnp.where((x > 0) & (agg_ref[jnp.maximum(x - 1, 0)] == label), 0.0, wxm)
        coarse = coarse + jnp.where((x < nx - 1) & (agg_ref[jnp.minimum(x + 1, nx - 1)] == label), 0.0, wxp)
        coarse = coarse + jnp.where(pltpu.roll(label, ny - 1, 0) == label, 0.0, wyp)
        coarse = coarse + jnp.where(pltpu.roll(label, 1, 0) == label, 0.0, wym)
        coarse = coarse + jnp.where(pltpu.roll(label, LANES - 1, 1) == label, 0.0, wzp)
        coarse = coarse + jnp.where(pltpu.roll(label, 1, 1) == label, 0.0, wzm)
        cbase_ref[x] = coarse
        ends_ref[0, pl.ds(x, 1), :] = jnp.min(label.astype(F32), axis=0, keepdims=True)
        ends_ref[1, pl.ds(x, 1), :] = jnp.max(label.astype(F32), axis=0, keepdims=True)

    planes(nx, assemble, unroll=2)
    low = jnp.min(ends_ref[0], axis=1, keepdims=True)
    high = jnp.max(ends_ref[1], axis=1, keepdims=True)
    low_ref[...] = jnp.broadcast_to(low, low_ref.shape).astype(jnp.int32)
    high_ref[...] = jnp.broadcast_to(high, high_ref.shape).astype(jnp.int32)


def rock_setup(
    b_ref, own_ref, wy_ref, base_ref, cbase_ref, edge_ref, ye_ref, yo_ref, par_ref,
    wyp_ref, wym_ref, dg_ref, z_ref, flow_ref, cc_ref, cell_ref, perm_ref, unperm_ref, count_ref,
    mxe_ref, mxo_ref, mye_ref, myo_ref,
    cv_ref, fv_ref, grid_ref, elo_ref, ehi_ref, ylo_ref, yhi_ref,
):
    nx, ny, _ = b_ref.shape
    fracs = own_ref.shape[0] // 3
    px, py = par_ref[0], par_ref[1]
    rate = -0.5 * mobility_rate

    even, odd = ye_ref[2 * nx :, :], yo_ref[2 * nx :, :]
    below, above = sided(py, even, odd)
    own = own_ref[...]

    def sources(i):
        part = slice(i * fracs, (i + 1) * fracs)
        return padded_rows([own[part], below[part], above[part]])

    cells = sources(0)
    active = jnp.broadcast_to((cells.T)[0:1, :], (8, LANES)) > 0.0
    hot = jnp.where(active, 1.0, 0.0)
    upto = jnp.where(iota((LANES, LANES), 0) <= iota((LANES, LANES), 1), 1.0, 0.0).astype(BF16)
    rank = mm(hot.astype(BF16), upto, (((1,), (0,)), ((), ())))
    place = jnp.where(active, rank, 0.0)[0:1, :].astype(jnp.int32)
    perm = jnp.where(place == iota((LANES, LANES), 0) + 1, 1.0, 0.0)
    perm_ref[...] = perm
    unperm_ref[...] = perm.T
    perm = perm.astype(BF16)
    count_ref[0] = jnp.sum(hot[0:1, :]).astype(jnp.int32)
    cell_ref[...] = reorder(perm, cells)
    cv_ref[...] = reorder(perm, sources(1))
    fv_ref[...] = reorder(perm, sources(2))
    host_spread(cell_ref, (cv_ref, fv_ref), groups_of(count_ref), grid_ref)

    k_lo, k_hi = sided(py, ye_ref[0:nx, :], yo_ref[0:nx, :])
    p_lo, p_hi = sided(py, ye_ref[nx : 2 * nx, :], yo_ref[nx : 2 * nx, :])
    elo_ref[...] = 2.0 * edge_ref[1] * (k_lo * jnp.exp(rate * p_lo)) / (edge_ref[0] + k_lo)
    ehi_ref[...] = 2.0 * edge_ref[3] * (k_hi * jnp.exp(rate * p_hi)) / (edge_ref[2] + k_hi)
    row = iota((ny, LANES), 0)

    def assemble(x):
        wyp = wy_ref[x]
        low = jnp.where(row == 0, elo_ref[pl.ds(x, 1), :], 0.0)
        high = jnp.where(row == ny - 1, ehi_ref[pl.ds(x, 1), :], 0.0)
        wyp_ref[x] = wyp + high
        wym_ref[x] = pltpu.roll(wyp, 1, 0) + low
        at = pl.ds(pl.multiple_of(x * ny, ny), ny)
        extra = grid_ref[at, 0:LANES] + low + high
        flow_ref[x] = grid_ref[at, LANES:]
        diag = base_ref[x] + extra
        dg_ref[x] = diag
        z = relaxation * b_ref[x] / diag
        z_ref[x] = z
        ylo_ref[pl.ds(x, 1), :] = z[0:1, :]
        yhi_ref[pl.ds(x, 1), :] = z[ny - 1 : ny, :]
        cc_ref[x] = cbase_ref[x] + extra

    planes(nx, assemble)
    write_layers(
        px, py, z_ref[0], z_ref[nx - 1], ylo_ref[...], yhi_ref[...], mxe_ref, mxo_ref, mye_ref, myo_ref
    )


def coarse_setup(cc_ref, agg_ref, low_ref, high_ref, cd_ref, sums_ref):
    sums = restrict(cc_ref, agg_ref, low_ref, high_ref, sums_ref)
    cd_ref[...] = jnp.where(iota((8, LANES), 1) < NAGG, sums, 1.0)


def fill_halo(vp_ref, v_ref, ylo_ref, yhi_ref, px, py, xe_ref, xo_ref, ye_ref, yo_ref):
    nx, ny, _ = v_ref.shape
    low, high = sided(px, xe_ref[...], xo_ref[...])
    vp_ref[0] = low
    vp_ref[nx + 1] = high

    def copy(x):
        vp_ref[x + 1] = v_ref[x]

    planes(nx, copy)
    low, high = sided(py, ye_ref[0:nx, :], yo_ref[0:nx, :])
    ylo_ref[...] = low
    yhi_ref[...] = high


def coarse_step(
    px, py, r_ref, z_ref, flow_of, agg_ref, weights, cd_ref, cell_ref, unperm_ref, scalars,
    p_ref, hv_ref, messages, vp_ref, ylo_ref, yhi_ref, s_ref, hc_ref, sums_ref,
):
    nx, ny, _ = z_ref.shape
    fracs = hv_ref.shape[0]
    count_ref, low_ref, high_ref = scalars

    def residual(x):
        v, near = near_sum(x, vp_ref, ylo_ref, yhi_ref, *weights)
        s_ref[x] = (1.0 - relaxation) * r_ref[x] + near + flow_of(x)

    planes(nx, residual)
    solved = restrict(s_ref, agg_ref, low_ref, high_ref, sums_ref) / cd_ref[...]

    def correct(x):
        z = vp_ref[x + 1]
        label = agg_ref[x]
        parts = [lane_pick(solved, label[h * 8 : (h + 1) * 8, :]) for h in range(ny // 8)]
        p = z + jnp.concatenate(parts, 0)
        p_ref[x] = p
        s_ref[x] = p
        ylo_ref[pl.ds(x, 1), :] = p[0:1, :]
        yhi_ref[pl.ds(x, 1), :] = p[ny - 1 : ny, :]

    planes(nx, correct)
    table = s_ref[...].reshape(nx * ny, LANES)
    host_fetch(table, cell_ref, groups_of(count_ref), hc_ref)
    values = reorder(unperm_ref[...].astype(BF16), hc_ref[...])
    hv_ref[...] = values[0:fracs]
    below, above = values[fracs : 2 * fracs], values[2 * fracs : 3 * fracs]
    write_layers(px, py, s_ref[0], s_ref[nx - 1], ylo_ref[...], yhi_ref[...], *messages)
    ye_ref, yo_ref = messages[2], messages[3]
    ye_ref[nx:, :] = jnp.where(py == 0, above, below)
    yo_ref[nx:, :] = jnp.where(py == 0, below, above)


def precond_first(
    b_ref, z_ref, flow_ref, agg_ref, wx_ref, wyp_ref, wym_ref, wzp_ref, cd_ref, cell_ref, unperm_ref,
    xe_ref, xo_ref, ye_ref, yo_ref, par_ref, count_ref, low_ref, high_ref,
    p_ref, hv_ref, mxe_ref, mxo_ref, mye_ref, myo_ref,
    vp_ref, ylo_ref, yhi_ref, s_ref, hc_ref, sums_ref,
):
    px, py = par_ref[0], par_ref[1]
    fill_halo(vp_ref, z_ref, ylo_ref, yhi_ref, px, py, xe_ref, xo_ref, ye_ref, yo_ref)
    coarse_step(
        px, py, b_ref, z_ref, lambda x: flow_ref[x], agg_ref, (wx_ref, wyp_ref, wym_ref, wzp_ref),
        cd_ref, cell_ref, unperm_ref, (count_ref, low_ref, high_ref), p_ref, hv_ref,
        (mxe_ref, mxo_ref, mye_ref, myo_ref), vp_ref, ylo_ref, yhi_ref, s_ref, hc_ref, sums_ref,
    )


def hosted_values(hv_ref, place_ref, py, ye_ref, yo_ref, nx, packed_ref, slot_ref, cpl_ref):
    fracs = hv_ref.shape[0]
    below, above = sided(py, ye_ref[nx:, :], yo_ref[nx:, :])
    packed_ref[...] = jnp.zeros(packed_ref.shape, F32)
    packed_ref[0:fracs, :] = hv_ref[...]
    packed_ref[PACK : PACK + fracs, :] = above
    packed_ref[2 * PACK : 2 * PACK + fracs, :] = below
    unpack_slots(place_ref, packed_ref, slot_ref, fracs)
    slot_ref[...] = slot_ref[...] * cpl_ref[...]


def image_first(
    p_ref, flow_ref, wx_ref, wyp_ref, wym_ref, wzp_ref, dg_ref, hv_ref, place_ref,
    fd_ref, q_ref, cpl_ref, cell_ref, xe_ref, xo_ref, ye_ref, yo_ref, par_ref,
    u_ref, z_ref, uf_ref, zn_ref, flux_ref, mxe_ref, mxo_ref, mye_ref, myo_ref,
    vp_ref, ylo_ref, yhi_ref, ylo_out_ref, yhi_out_ref, slot_ref, spread_ref, packed_ref,
):
    nx, ny, _ = p_ref.shape
    fracs, width = q_ref.shape
    tiles = width // LANES
    px, py = par_ref[0], par_ref[1]
    fill_halo(vp_ref, p_ref, ylo_ref, yhi_ref, px, py, xe_ref, xo_ref, ye_ref, yo_ref)
    weights = (wx_ref, wyp_ref, wym_ref, wzp_ref)

    def image(x):
        v, near = near_sum(x, vp_ref, ylo_ref, yhi_ref, *weights)
        diag = dg_ref[x]
        u = diag * v - near - flow_ref[x]
        u_ref[x] = u
        z = relaxation * u / diag
        z_ref[x] = z
        ylo_out_ref[pl.ds(x, 1), :] = z[0:1, :]
        yhi_out_ref[pl.ds(x, 1), :] = z[ny - 1 : ny, :]

    planes(nx, image)

    hosted_values(hv_ref, place_ref, py, ye_ref, yo_ref, nx, packed_ref, slot_ref, cpl_ref)
    slab_spread(cell_ref, slot_ref, spread_ref, tiles)
    for t in range(tiles):
        out = q_ref[:, tile(t)] - spread_ref[pl.ds(t, fracs, stride=tiles), :]
        uf_ref[:, tile(t)] = out
        zn_ref[:, tile(t)] = relaxation * out / fd_ref[:, tile(t)]
    slot_ref[...] = cpl_ref[...] * slab_pick(lambda t: zn_ref[:, tile(t)], cell_ref[...], tiles)
    pack_slots(place_ref, (slot_ref,), (packed_ref,), fracs)
    flux_ref[...] = packed_ref[0:fracs, :]

    write_layers(
        px, py, z_ref[0], z_ref[nx - 1], ylo_out_ref[...], yhi_out_ref[...], mxe_ref, mxo_ref, mye_ref, myo_ref
    )
    mye_ref[nx:, :], myo_ref[nx:, :] = directed(py == 0, packed_ref, fracs)


def precond_second(
    u_ref, z_ref, flux_ref, agg_ref, wx_ref, wyp_ref, wym_ref, wzp_ref, cd_ref, cell_ref, perm_ref, unperm_ref,
    xe_ref, xo_ref, ye_ref, yo_ref, par_ref, count_ref, low_ref, high_ref,
    p_ref, hv_ref, flow_ref, mxe_ref, mxo_ref, mye_ref, myo_ref,
    vp_ref, ylo_ref, yhi_ref, s_ref, hc_ref, fv_ref, grid_ref, sums_ref,
):
    nx, ny, _ = z_ref.shape
    px, py = par_ref[0], par_ref[1]
    fill_halo(vp_ref, z_ref, ylo_ref, yhi_ref, px, py, xe_ref, xo_ref, ye_ref, yo_ref)
    below, above = sided(py, ye_ref[nx:, :], yo_ref[nx:, :])
    fv_ref[...] = reorder(perm_ref[...].astype(BF16), padded_rows([flux_ref[...], below, above]))
    host_spread(cell_ref, (fv_ref,), groups_of(count_ref), grid_ref)

    def flow_of(x):
        flow = grid_ref[pl.ds(pl.multiple_of(x * ny, ny), ny), :]
        flow_ref[x] = flow
        return flow

    coarse_step(
        px, py, u_ref, z_ref, flow_of, agg_ref, (wx_ref, wyp_ref, wym_ref, wzp_ref),
        cd_ref, cell_ref, unperm_ref, (count_ref, low_ref, high_ref), p_ref, hv_ref,
        (mxe_ref, mxo_ref, mye_ref, myo_ref), vp_ref, ylo_ref, yhi_ref, s_ref, hc_ref, sums_ref,
    )


def frac_second(
    fd_ref, al_ref, ac_ref, z_ref, xc_ref, pairs_ref,
    q_ref,
    cross_ref, hot_ref,
):
    fracs, width = z_ref.shape
    tiles = width // LANES
    rows_at, lane_at = cross_place(pairs_ref, fracs)
    cross_hot(rows_at, hot_ref)
    ends = cross_pick(lambda t: z_ref[:, tile(t)], tiles, hot_ref, lane_at)
    cross_spread(xc_ref[...] * ends_swapped(ends), hot_ref, lane_at, cross_ref)
    first = iota((fracs, LANES), 1) < FSIDE
    carry = stencil_start(z_ref, fracs)
    for t in range(tiles):
        out, carry = frac_stencil(t, tiles, fd_ref, al_ref, ac_ref, z_ref, first, carry)
        q_ref[:, tile(t)] = out - cross_ref[t * fracs : (t + 1) * fracs, :]


def sums_of(rock, frac):
    return jnp.sum(rock, axis=0, keepdims=True) + jnp.sum(frac, axis=0, keepdims=True)


def dots_first(b_ref, u_ref, bf_ref, uf_ref, sums_ref):
    nx, ny, _ = b_ref.shape
    fracs, width = bf_ref.shape

    def products(b, u, sums):
        return tuple(s + t for s, t in zip(sums, (b * b, u * b, u * u)))

    def plane(x, sums):
        return products(b_ref[x], u_ref[x], sums)

    rock = lax.fori_loop(0, nx, plane, tuple(jnp.zeros((ny, LANES), F32) for _ in range(3)), unroll=4)
    frac = tuple(jnp.zeros((fracs, LANES), F32) for _ in range(3))
    for t in range(width // LANES):
        frac = products(bf_ref[:, tile(t)], uf_ref[:, tile(t)], frac)
    sub = iota((8, LANES), 0)
    table = jnp.zeros((8, LANES), F32)
    for i in range(3):
        table = jnp.where(sub == i, sums_of(rock[i], frac[i]), table)
    sums_ref[...] = table


def image_second(
    p_ref, flow_ref, wx_ref, wyp_ref, wym_ref, wzp_ref, dg_ref, b_ref, u_ref, hv_ref, place_ref,
    q_ref, cpl_ref, cell_ref, bf_ref, uf_ref, first_ref, xe_ref, xo_ref, ye_ref, yo_ref, par_ref,
    sums_ref,
    vp_ref, ylo_ref, yhi_ref, slot_ref, spread_ref, packed_ref,
):
    nx, ny, _ = p_ref.shape
    fracs, width = q_ref.shape
    tiles = width // LANES
    px, py = par_ref[0], par_ref[1]
    fill_halo(vp_ref, p_ref, ylo_ref, yhi_ref, px, py, xe_ref, xo_ref, ye_ref, yo_ref)
    weights = (wx_ref, wyp_ref, wym_ref, wzp_ref)

    def image(x, sums):
        v, near = near_sum(x, vp_ref, ylo_ref, yhi_ref, *weights)
        w = dg_ref[x] * v - near - flow_ref[x]
        return tuple(s + t for s, t in zip(sums, (w * b_ref[x], w * u_ref[x], w * w)))

    rock = lax.fori_loop(0, nx, image, tuple(jnp.zeros((ny, LANES), F32) for _ in range(3)), unroll=4)
    hosted_values(hv_ref, place_ref, py, ye_ref, yo_ref, nx, packed_ref, slot_ref, cpl_ref)
    slab_spread(cell_ref, slot_ref, spread_ref, tiles)
    frac = [jnp.zeros((fracs, LANES), F32) for _ in range(3)]
    for t in range(tiles):
        w = q_ref[:, tile(t)] - spread_ref[pl.ds(t, fracs, stride=tiles), :]
        frac = [s + t_ for s, t_ in zip(frac, (w * bf_ref[:, tile(t)], w * uf_ref[:, tile(t)], w * w))]
    sub = iota((8, LANES), 0)
    table = first_ref[...]
    for i in range(3):
        table = jnp.where(sub == i + 3, sums_of(rock[i], frac[i]), table)
    table = jnp.concatenate([table, jnp.zeros((LANES - 8, LANES), F32)], 0)
    ones = jnp.ones((8, LANES), BF16)
    row = sum(mm(ones, part, NT) for part in thirds(table))[0:1, :]
    sums_ref[...] = jnp.broadcast_to(row, sums_ref.shape)


def finish(all_ref, p_ref, q_ref, pf_ref, qf_ref, rock_ref, frac_ref, res_ref):
    total = jnp.sum(all_ref[...], axis=0, keepdims=True)
    total = jnp.broadcast_to(total, (8, LANES))
    bb, ub, uu, wb, wu, ww = (
        lane_pick(total, jnp.full((8, LANES), i, jnp.int32)) for i in range(6)
    )
    norm2 = bb + epsilon
    norm = jnp.sqrt(norm2)
    h00 = ub / norm2
    n1 = jnp.maximum(uu - 2.0 * h00 * ub + h00 * h00 * bb, 0.0) / norm2
    h10 = jnp.sqrt(n1 + epsilon)
    h01 = (wb - h00 * ub) / (norm2 * h10)
    h11 = (wu - h00 * wb - h00 * uu + h00 * h00 * ub) / (norm2 * h10 * h10)
    square = (ww - 2.0 * h00 * wu + h00 * h00 * uu) / (norm2 * h10 * h10)
    v00 = bb / norm2
    v11 = n1 / (h10 * h10)
    v01 = (ub - h00 * bb) / (norm2 * h10)
    n2 = square + h01 * h01 * (v00 - 2.0) + h11 * h11 * (v11 - 2.0) + 2.0 * h01 * h11 * v01
    h21 = jnp.sqrt(jnp.maximum(n2, epsilon * square) + epsilon)
    r0 = jnp.sqrt(h00 * h00 + h10 * h10)
    c0, s0 = h00 / r0, h10 / r0
    top = c0 * h01 + s0 * h11
    low = c0 * h11 - s0 * h01
    r1 = jnp.sqrt(low * low + h21 * h21)
    c1, s1 = low / r1, h21 / r1
    g0, g1 = c0 * norm, -s0 * norm
    y1 = c1 * g1 / r1
    y0 = (g0 - top * y1) / r0
    residual = jnp.abs(s1 * g1)
    beta = y1 / (norm * h10)
    alpha = y0 / norm - h00 * beta
    res_ref[0, 0] = residual[0, 0]
    nx, ny, _ = p_ref.shape
    alpha_y, beta_y = alpha[0:1, :], beta[0:1, :]

    def rock(x):
        rock_ref[x] = alpha_y * p_ref[x] + beta_y * q_ref[x]

    planes(nx, rock)
    for t in range(pf_ref.shape[1] // LANES):
        frac_ref[:, tile(t)] = alpha_y * pf_ref[:, tile(t)] + beta_y * qf_ref[:, tile(t)]


def local(
    rock_rhs,
    frac_rhs,
    perm,
    storage,
    pressure,
    frac_perm,
    frac_storage,
    frac_pressure,
    couple_geom,
    couple_count,
    couple_frac_cell,
    couple_rock_cell,
    host_offset,
    cross_pairs,
    cross_geom,
    aggregates,
):
    nx, ny, nz = rock_rhs.shape
    fracs, width = frac_rhs.shape
    pairs = cross_pairs.shape[1]
    tiles = width // LANES
    cube, slab, slots = shaped(nx, ny, nz), shaped(fracs, width), shaped(fracs, LANES)
    gx, gy = lax.axis_index("gx"), lax.axis_index("gy")
    parity = jnp.stack([gx % 2, gy % 2]).astype(jnp.int32)
    vcube = pltpu.VMEM((nx, ny, nz), F32)
    vpad = pltpu.VMEM((nx + 2, ny, nz), F32)
    vside = pltpu.VMEM((nx, nz), F32)
    vhost = pltpu.VMEM((LANES, LANES), F32)
    vcross = pltpu.VMEM((fracs * tiles, LANES), F32)
    vhot = pltpu.VMEM((fracs * tiles, 2 * pairs), BF16)
    vslots = pltpu.VMEM((fracs, LANES), F32)

    even_x = gx % 2 == 0
    x_lo = jnp.concatenate([a[0] for a in (perm, pressure)], 0)
    x_hi = jnp.concatenate([a[nx - 1] for a in (perm, pressure)], 0)
    x_even, x_odd = exchange(jnp.where(even_x, x_hi, x_lo), jnp.where(even_x, x_lo, x_hi), "gx")

    vslab = pltpu.VMEM((fracs, width), F32)
    vpack = pltpu.VMEM((3 * PACK, LANES), F32)
    message = shaped(2 * nx + 3 * fracs, LANES)
    al, ac, fd, zf, cpl, xc, own, y_even, y_odd, place = call(
        frac_setup,
        [slab, slab, slab, slab, slots, shaped(1, 2 * pairs), shaped(3 * fracs, LANES), message, message]
        + [shaped(fracs, dtype=jnp.int32)],
        [
            frac_rhs, frac_perm, frac_storage, frac_pressure, couple_geom, couple_frac_cell, couple_rock_cell,
            cross_pairs, cross_geom.reshape(1, pairs), couple_count, host_offset, perm, pressure, parity,
        ],
        [vcross, vcross, vhot] + [vslab] * 9 + [pltpu.VMEM((4, nx, nz), F32), vslots, vslots] + [vpack] * 3
        + [pltpu.SemaphoreType.DMA((12,))],
        smem_in=(9, 10, 13),
        hbm_in=(0, 1, 2, 3, 11, 12),
        smem_out=(9,),
        hbm_out=(0, 1, 2, 3),
        limit=62,
    )
    y_even, y_odd = exchange(y_even, y_odd, "gy")

    layers = [shaped(ny, nz), shaped(ny, nz)]
    count_shape = shaped(1, dtype=jnp.int32)
    host_shape = shaped(LANES, LANES)
    range_shape = shaped(nx, LANES, dtype=jnp.int32)
    wx, wy, wzp, base, cbase, edge, low, high = call(
        rock_faces,
        [shaped(nx + 1, ny, nz), cube, cube, cube, cube, shaped(4, nx, nz), range_shape, range_shape],
        [perm, pressure, storage, aggregates, x_even, x_odd, parity],
        [vpad, vpad, pltpu.VMEM((2, nx, nz), F32)],
        smem_in=(6,),
    )
    wyp, wym, dg, z0, flow0, cc, cells, pack, unpack, count, xe, xo, ye, yo = call(
        rock_setup,
        [cube] * 6 + [host_shape] * 3 + [count_shape] + layers + [shaped(nx, nz)] * 2,
        [rock_rhs, own, wy, base, cbase, edge, y_even, y_odd, parity],
        [vhost, vhost, pltpu.VMEM((nx * ny, 2 * LANES), F32), vside, vside, vside, vside],
        smem_in=(8,),
        smem_out=(9,),
    )
    vsums = pltpu.VMEM((NAGG + CHUNK, 8, LANES), F32)
    weights = [wx, wyp, wym, wzp]
    xe, xo = exchange(xe, xo, "gx")
    ye, yo = exchange(ye, yo, "gy")
    (cd,) = call(
        coarse_setup, [shaped(8, LANES)], [cc, aggregates, low, high], [vsums], smem_in=(2, 3)
    )
    p0, hv, xe, xo, ye, yo = call(
        precond_first,
        [cube, slots] + layers + [shaped(nx + fracs, nz)] * 2,
        [rock_rhs, z0, flow0, aggregates] + weights + [cd, cells, unpack, xe, xo, ye, yo, parity, count, low, high],
        [vpad, vside, vside, vcube, vhost, vsums],
        smem_in=(15, 16, 17, 18),
    )
    xe, xo = exchange(xe, xo, "gx")
    ye, yo = exchange(ye, yo, "gy")
    (q0,) = call(frac_second, [slab], [fd, al, ac, zf, xc, cross_pairs], [vcross, vhot])
    u0, z1, uf0, zf1, flux1, xe, xo, ye, yo = call(
        image_first,
        [cube, cube, slab, slab, slots] + layers + [shaped(nx + fracs, nz)] * 2,
        [p0, flow0] + weights + [dg, hv, place, fd, q0, cpl, couple_frac_cell, xe, xo, ye, yo, parity],
        [vpad, vside, vside, vside, vside, vslots, vcross, vpack],
        smem_in=(8, 17),
    )
    xe, xo = exchange(xe, xo, "gx")
    ye, yo = exchange(ye, yo, "gy")
    (q1,) = call(frac_second, [slab], [fd, al, ac, zf1, xc, cross_pairs], [vcross, vhot])
    p1, hv, flow1, xe, xo, ye, yo = call(
        precond_second,
        [cube, slots, cube] + layers + [shaped(nx + fracs, nz)] * 2,
        [u0, z1, flux1, aggregates] + weights + [cd, cells, pack, unpack, xe, xo, ye, yo, parity, count, low, high],
        [vpad, vside, vside, vcube, vhost, vhost, pltpu.VMEM((nx * ny, LANES), F32), vsums],
        smem_in=(16, 17, 18, 19),
    )
    xe, xo = exchange(xe, xo, "gx")
    ye, yo = exchange(ye, yo, "gy")
    (first,) = call(dots_first, [shaped(8, LANES)], [rock_rhs, u0, frac_rhs, uf0])
    devices = lax.axis_size("gx") * lax.axis_size("gy")
    (sums,) = call(
        image_second,
        [shaped(devices, LANES)],
        [p1, flow1] + weights + [dg, rock_rhs, u0, hv, place, q1, cpl, couple_frac_cell, frac_rhs, uf0, first, xe, xo, ye, yo, parity],
        [vpad, vside, vside, vslots, vcross, vpack],
        smem_in=(10, 21),
    )
    gathered = lax.all_to_all(sums, ("gx", "gy"), 0, 0, tiled=True)
    rock_update, frac_update, residual = call(
        finish,
        [cube, slab, shaped(1, 1)],
        [gathered, p0, p1, zf, zf1],
        smem_out=(2,),
    )
    return rock_update, frac_update, residual.reshape(())


def solution(mesh):
    placed = (
        P("gx", "gy", None),
        P(("gx", "gy"), None),
        P("gx", "gy", None),
        P("gx", "gy", None),
        P("gx", "gy", None),
        P(("gx", "gy"), None),
        P(("gx", "gy"), None),
        P(("gx", "gy"), None),
        P(("gx", "gy"), None),
        P(("gx", "gy")),
        P(("gx", "gy"), None),
        P(("gx", "gy"), None),
        P(("gx", "gy")),
        P(None, ("gx", "gy")),
        P(("gx", "gy")),
        P("gx", "gy", None),
    )
    return jax.shard_map(
        local,
        mesh=mesh,
        in_specs=placed,
        out_specs=(P("gx", "gy", None), P(("gx", "gy"), None), P()),
        check_vma=False,
    )
```
